32 devices in a mesh: fsdp: 4 (over x, core), ctx: 4 (over z), tensor: 2 (over y).
Axes of the slice: x: 2, y: 2, z: 4, core: 2. Of those that a mesh axis runs over, the one named last changes fastest.
Arguments:
- block_input: bfloat16 [4096, 2048], P(('fsdp', 'ctx')), may hold values from -6 to 6
- seq_lengths: int32 [4, 3], P('fsdp'), may hold values from 1 to 512, 1024 in all within a row
- attn_gain: bfloat16 [2048], P('fsdp'), may hold values from 0.5 to 1.5
- w_query: bfloat16 [2048, 2048], P('fsdp', 'tensor'), as said below
- w_key: bfloat16 [2048, 512], P('fsdp', 'tensor'), as said below
- w_value: bfloat16 [2048, 512], P('fsdp', 'tensor'), may hold values from -0.125 to 0.125
- w_output: bfloat16 [2048, 2048], P('tensor', 'fsdp'), may hold values from -2 to 2
- mlp_gain: bfloat16 [2048], P('fsdp'), may hold values from 0.5 to 1.5
- w_gate: bfloat16 [2048, 8192], P('fsdp', 'tensor'), may hold values from -0.125 to 0.125
- w_up: bfloat16 [2048, 8192], P('fsdp', 'tensor'), may hold values from -0.125 to 0.125
- w_down: bfloat16 [8192, 2048], P('tensor', 'fsdp'), may hold values from -0.0625 to 0.0625
- cotangent: bfloat16 [4096, 2048], P(('fsdp', 'ctx')), may hold values from -6 to 6
Outputs:
- block_output: bfloat16 [4096, 2048], P(('fsdp', 'ctx'))
- input_grad: float32 [4096, 2048], P(('fsdp', 'ctx'))
- attn_gain_grad: float32 [2048], P('fsdp')
- query_grad: float32 [2048, 2048], P('fsdp', 'tensor')
- key_grad: float32 [2048, 512], P('fsdp', 'tensor')
- value_grad: float32 [2048, 512], P('fsdp', 'tensor')
- output_grad: float32 [2048, 2048], P('tensor', 'fsdp')
- mlp_gain_grad: float32 [2048], P('fsdp')
- gate_grad: float32 [2048, 8192], P('fsdp', 'tensor')
- up_grad: float32 [2048, 8192], P('fsdp', 'tensor')
- down_grad: float32 [8192, 2048], P('tensor', 'fsdp')
The draws below stay inside these ranges and needn't reach their ends.
Inputs may be any that keep to these rules, and one draw needn't show every extreme that they name: `seq_lengths`: each row sums to 1024, and its largest entry is exactly 512. `w_query`: a projection matrix. `w_key`: a projection matrix.
All inputs are finite; a program needn't handle non-finite values.
Results may differ from the reference program's by a relative error of at most 0.02.
Values may be sent and summed in bfloat16 or wider, within the bound.
No kernel may reach another device: no remote copies, remote signals or barrier semaphores. Data moves between devices by JAX's collectives and lax.ppermute only.
A program may use at most 320 MiB of HBM per device.

```python
import math
import jax
import jax.numpy as jnp
import numpy as np
from jax import lax

D = 2048
H = 32
KV = 8
HD = 64
FF = 8192
NSEQ = 3
GROUP_TOK = 1024
MAXLEN = 512
TOKENS = 4096
N_FSDP = 4


def key_matrix(key):
    return jax.random.normal(jax.random.fold_in(key, 7), (D, KV * HD), jnp.float32) * D ** (-0.5)


def draw_w_key(key, part):
    return key_matrix(key).astype(jnp.bfloat16)


def draw_w_query(key, part):
    base = jax.random.normal(jax.random.fold_in(key, 11), (D, H * HD), jnp.float32) * D ** (-0.5)
    return base.astype(jnp.bfloat16)


def block_levels(stream_key, dims, split, smallest, top_value):
    loudness = 1.0
    for dim, blocks in split:
        heights = jax.random.uniform(jax.random.fold_in(jax.random.fold_in(stream_key, 6), dim), (blocks,), jnp.float32, smallest / len(split), top_value / len(split))
        loudness = loudness * jnp.repeat(jnp.exp(heights), dims[dim] // blocks).reshape((-1,) + (1,) * (len(dims) - 1 - dim))
    return loudness


def split_up(amount, total, most, lean):
    portions = [(1 << 20) // math.isqrt(grade ** lean) + 1 for grade in range(2, amount + 1)]
    surplus, counts = total - most - (amount - 1), [1] * (amount - 1)
    while surplus > 0:
        movable = [i for i in range(amount - 1) if counts[i] < most]
        pool, budget = sum([portions[i] for i in movable]), surplus
        for i in movable:
            more = min(most - counts[i], max(1, budget * portions[i] // pool), surplus)
            counts[i] = counts[i] + more
            surplus = surplus - more
    return np.array([most] + counts)


def uneven_parts(own_key, amount, total, reach, skew):
    if amount == 2:
        one = jax.random.randint(own_key, (), max(1, total - reach), min(reach, total - 1) + 1)
        return jnp.stack([one, total - one])
    lengths = jnp.asarray(split_up(amount, total, reach, skew), jnp.int32)
    couples = (amount - 1) // 2
    donor, sink = lengths[1:1 + 2 * couples:2], lengths[2:2 + 2 * couples:2]
    margin = jnp.minimum(donor - 1, reach - sink)
    moved = jax.random.randint(jax.random.fold_in(own_key, 1), (couples,), 0, 1 << 20) % (margin + 1)
    lengths = lengths.at[1:1 + 2 * couples:2].set(donor - moved).at[2:2 + 2 * couples:2].set(sink + moved)
    return lengths[jax.random.permutation(jax.random.fold_in(own_key, 2), amount)]


def noise(own_key, shape, width, reach, shards=(), held_as=jnp.bfloat16):
    gain = block_levels(own_key, shape, shards, -0.22, 0.18) if shards else 1.0
    drawn = jax.random.normal(own_key, shape, jnp.float32) * width * gain
    return jnp.minimum(jnp.maximum(drawn, -reach), reach).astype(held_as)


def setup_inputs(seed: int = 0) -> dict:
    key_list = jax.random.split(jax.random.key(seed), 13)
    block_input = noise(key_list[0], (TOKENS, D), 1.0, 6.0, ((0, 16),))
    seq_lengths = jax.vmap(lambda own: uneven_parts(own, NSEQ, GROUP_TOK, MAXLEN, 2))(jax.random.split(key_list[1], N_FSDP)).reshape((N_FSDP, NSEQ)).astype(jnp.int32)
    attn_gain = jnp.clip(1.0 + 0.1 * jax.random.normal(key_list[2], (D,), jnp.float32), 0.5, 1.5).astype(jnp.bfloat16)
    w_query = draw_w_query(jax.random.fold_in(key_list[12], 71), 0)
    w_key = draw_w_key(jax.random.fold_in(key_list[12], 71), 0)
    w_value = noise(key_list[5], (D, KV * HD), D ** -0.5, 0.125, ((0, 4), (1, 2)))
    w_output = noise(key_list[6], (H * HD, D), (max(H * HD // 256, 4)) ** -0.5, 2.0, ((0, 2), (1, 4)))
    mlp_gain = jnp.clip(1.0 + 0.1 * jax.random.normal(key_list[7], (D,), jnp.float32), 0.5, 1.5).astype(jnp.bfloat16)
    w_gate = noise(key_list[8], (D, FF), D ** -0.5, 0.125, ((0, 4), (1, 2)))
    w_up = noise(key_list[9], (D, FF), D ** -0.5, 0.125, ((0, 4), (1, 2)))
    w_down = noise(key_list[10], (FF, D), FF ** -0.5, 0.0625, ((0, 2), (1, 4)))
    cotangent = noise(key_list[11], (TOKENS, D), 1.0, 6.0, ((0, 16),))
    return dict(block_input=block_input, seq_lengths=seq_lengths, attn_gain=attn_gain, w_query=w_query, w_key=w_key, w_value=w_value, w_output=w_output, mlp_gain=mlp_gain, w_gate=w_gate, w_up=w_up, w_down=w_down, cotangent=cotangent)


eps_norm = 1e-05
rope_base = 500000.0

def layout(lengths_row, token_index):
    seq_ends = jnp.cumsum(lengths_row)
    passed = (token_index[:, None] >= seq_ends[None, :]).astype(jnp.int32)
    segment = lax.optimization_barrier(jnp.sum(passed, axis=1))
    seq_start = lax.optimization_barrier(jnp.sum(passed * lengths_row[None, :], axis=1))
    return (segment, token_index - seq_start)

def rope_tables(position):
    half_width = HD // 2
    frequency = rope_base ** (-jnp.arange(half_width, dtype=jnp.float32) / half_width)
    angles = position.astype(jnp.float32)[:, None] * frequency[None, :]
    return (jnp.cos(angles), jnp.sin(angles))

def rotate(vectors, cosine_table, sine_table, direction):
    half_width = HD // 2
    first_half = vectors[..., :half_width]
    second = vectors[..., half_width:]
    cos_rows = cosine_table[:, None, :]
    sin_rows = direction * sine_table[:, None, :]
    return jnp.concatenate([first_half * cos_rows - second * sin_rows, second * cos_rows + first_half * sin_rows], axis=-1)

def norm_forward(rows_wide):
    inv_rms = lax.rsqrt(lax.optimization_barrier(jnp.mean(rows_wide * rows_wide, axis=-1, keepdims=True)) + eps_norm)
    return (rows_wide * inv_rms, inv_rms)

def norm_backward(delta_rows, unit_rows, inv_rms, gain_weights):
    scaled = gain_weights.astype(jnp.float32)[None, :] * delta_rows
    gain_term = lax.optimization_barrier(jnp.sum(delta_rows * unit_rows, axis=0))
    back_term = inv_rms * (scaled - unit_rows * lax.optimization_barrier(jnp.mean(scaled * unit_rows, axis=-1, keepdims=True)))
    return (gain_term, back_term)

def head_forward(queries, key_rows, values, allowed, score_scale):
    scores = jnp.einsum('tgd,sd->gts', queries.astype(jnp.float32), key_rows.astype(jnp.float32)) * score_scale
    masked = jnp.where(allowed[None], scores, -1e+30)
    row_max = lax.optimization_barrier(jnp.max(masked, axis=-1, keepdims=True))
    exp_total = lax.optimization_barrier(jnp.sum(jnp.where(allowed[None], jnp.exp(masked - row_max), 0.0), axis=-1, keepdims=True))
    log_total = row_max + jnp.log(exp_total)
    attn_prob = jnp.where(allowed[None], jnp.exp(scores - log_total), 0.0).astype(jnp.bfloat16)
    attended = jnp.einsum('gts,sd->tgd', attn_prob.astype(jnp.float32), values.astype(jnp.float32)).astype(jnp.bfloat16)
    return (attended, log_total[..., 0])

def head_backward(queries, key_rows, values, log_total, out_delta, inner_rows, allowed, score_scale):
    scores = jnp.einsum('tgd,sd->gts', queries.astype(jnp.float32), key_rows.astype(jnp.float32)) * score_scale
    attn_prob = jnp.where(allowed[None], jnp.exp(scores - log_total[..., None]), 0.0)
    prob_delta = jnp.einsum('tgd,sd->gts', out_delta.astype(jnp.float32), values.astype(jnp.float32))
    score_delta = (attn_prob * (prob_delta - inner_rows[..., None]) * score_scale).astype(jnp.bfloat16)
    query_back = jnp.einsum('gts,sd->tgd', score_delta.astype(jnp.float32), key_rows.astype(jnp.float32))
    key_back = jnp.einsum('gts,tgd->sd', score_delta.astype(jnp.float32), queries.astype(jnp.float32))
    value_back = jnp.einsum('gts,tgd->sd', attn_prob.astype(jnp.bfloat16).astype(jnp.float32), out_delta.astype(jnp.float32))
    return (query_back, key_back, value_back)

def reference(block_input, seq_lengths, attn_gain, w_query, w_key, w_value, w_output, mlp_gain, w_gate, w_up, w_down, cotangent):
    group_rows = GROUP_TOK
    head_share = H // KV
    score_scale = 1.0 / math.sqrt(HD)
    token_index = jnp.arange(group_rows, dtype=jnp.int32)

    def one_group(totals, operands):
        rows_in, rows_cot, lengths_row = operands
        segment, position = layout(lengths_row, token_index)
        allowed = (segment[:, None] == segment[None, :]) & (token_index[None, :] <= token_index[:, None])
        cosine_table, sine_table = rope_tables(position)
        input_wide = rows_in.astype(jnp.float32)
        unit_one, rstd_one = norm_forward(input_wide)
        normed_one = (unit_one * attn_gain.astype(jnp.float32)[None, :]).astype(jnp.bfloat16)
        query_pre = jnp.dot(normed_one, w_query, preferred_element_type=jnp.float32).reshape(group_rows, H, HD)
        key_pre = jnp.dot(normed_one, w_key, preferred_element_type=jnp.float32).reshape(group_rows, KV, HD)
        value_rows = jnp.dot(normed_one, w_value, preferred_element_type=jnp.float32).astype(jnp.bfloat16)
        query_rot = rotate(query_pre, cosine_table, sine_table, 1.0).astype(jnp.bfloat16)
        key_rot = rotate(key_pre, cosine_table, sine_table, 1.0).astype(jnp.bfloat16)
        query_heads = jnp.moveaxis(query_rot.reshape(group_rows, KV, head_share, HD), 1, 0)
        key_heads = jnp.moveaxis(key_rot, 1, 0)
        value_heads = jnp.moveaxis(value_rows.reshape(group_rows, KV, HD), 1, 0)
        attended, log_total = lax.map(lambda parts_h: head_forward(parts_h[0], parts_h[1], parts_h[2], allowed, score_scale), (query_heads, key_heads, value_heads))
        attended_rows = jnp.moveaxis(attended, 0, 1).reshape(group_rows, H * HD)
        residual = input_wide + jnp.dot(attended_rows, w_output, preferred_element_type=jnp.float32)
        unit_two, rstd_two = norm_forward(residual)
        normed_two = (unit_two * mlp_gain.astype(jnp.float32)[None, :]).astype(jnp.bfloat16)
        gate_pre = jnp.dot(normed_two, w_gate, preferred_element_type=jnp.float32)
        up_pre = jnp.dot(normed_two, w_up, preferred_element_type=jnp.float32)
        sigmoid_gate = jax.nn.sigmoid(gate_pre)
        silu_gate = gate_pre * sigmoid_gate
        activation = (silu_gate * up_pre).astype(jnp.bfloat16)
        block_output = (residual + jnp.dot(activation, w_down, preferred_element_type=jnp.float32)).astype(jnp.bfloat16)
        act_delta = jnp.dot(rows_cot, w_down.T, preferred_element_type=jnp.float32)
        silu_slope = sigmoid_gate * (1.0 + gate_pre * (1.0 - sigmoid_gate))
        gate_delta = (act_delta * up_pre * silu_slope).astype(jnp.bfloat16)
        up_delta = (act_delta * silu_gate).astype(jnp.bfloat16)
        down_term = jnp.dot(activation.T, rows_cot, preferred_element_type=jnp.float32)
        gate_term = jnp.dot(normed_two.T, gate_delta, preferred_element_type=jnp.float32)
        up_term = jnp.dot(normed_two.T, up_delta, preferred_element_type=jnp.float32)
        normed_two_delta = jnp.dot(gate_delta, w_gate.T, preferred_element_type=jnp.float32) + jnp.dot(up_delta, w_up.T, preferred_element_type=jnp.float32)
        gain_two_term, residual_back = norm_backward(normed_two_delta, unit_two, rstd_two, mlp_gain)
        residual_delta = rows_cot.astype(jnp.float32) + residual_back
        residual_low = residual_delta.astype(jnp.bfloat16)
        output_term = jnp.dot(attended_rows.T, residual_low, preferred_element_type=jnp.float32)
        attended_delta = jnp.dot(residual_low, w_output.T, preferred_element_type=jnp.float32).astype(jnp.bfloat16)
        delta_heads = jnp.moveaxis(attended_delta.reshape(group_rows, KV, head_share, HD), 1, 0)
        inner_rows = jnp.moveaxis(lax.optimization_barrier(jnp.sum(attended.astype(jnp.float32) * delta_heads.astype(jnp.float32), axis=-1)), 2, 1)
        query_back, key_back, value_back = lax.map(lambda parts_h: head_backward(parts_h[0], parts_h[1], parts_h[2], parts_h[3], parts_h[4], parts_h[5], allowed, score_scale), (query_heads, key_heads, value_heads, log_total, delta_heads, inner_rows))
        query_delta = rotate(jnp.moveaxis(query_back, 0, 1).reshape(group_rows, H, HD), cosine_table, sine_table, -1.0).reshape(group_rows, H * HD).astype(jnp.bfloat16)
        key_delta = rotate(jnp.moveaxis(key_back, 0, 1), cosine_table, sine_table, -1.0).reshape(group_rows, KV * HD).astype(jnp.bfloat16)
        value_delta = jnp.moveaxis(value_back, 0, 1).reshape(group_rows, KV * HD).astype(jnp.bfloat16)
        query_term = jnp.dot(normed_one.T, query_delta, preferred_element_type=jnp.float32)
        key_term = jnp.dot(normed_one.T, key_delta, preferred_element_type=jnp.float32)
        value_term = jnp.dot(normed_one.T, value_delta, preferred_element_type=jnp.float32)
        normed_one_delta = jnp.dot(query_delta, w_query.T, preferred_element_type=jnp.float32) + jnp.dot(key_delta, w_key.T, preferred_element_type=jnp.float32) + jnp.dot(value_delta, w_value.T, preferred_element_type=jnp.float32)
        gain_one_term, input_back = norm_backward(normed_one_delta, unit_one, rstd_one, attn_gain)
        input_grad = residual_delta + input_back
        new_totals = (totals[0] + gain_one_term, totals[1] + query_term, totals[2] + key_term, totals[3] + value_term, totals[4] + output_term, totals[5] + gain_two_term, totals[6] + gate_term, totals[7] + up_term, totals[8] + down_term)
        return (new_totals, (block_output, input_grad))
    zero_totals = (jnp.zeros((D,), jnp.float32), jnp.zeros((D, H * HD), jnp.float32), jnp.zeros((D, KV * HD), jnp.float32), jnp.zeros((D, KV * HD), jnp.float32), jnp.zeros((H * HD, D), jnp.float32), jnp.zeros((D,), jnp.float32), jnp.zeros((D, FF), jnp.float32), jnp.zeros((D, FF), jnp.float32), jnp.zeros((FF, D), jnp.float32))
    totals, stacked = lax.scan(one_group, zero_totals, (block_input.reshape(N_FSDP, GROUP_TOK, D), cotangent.reshape(N_FSDP, GROUP_TOK, D), seq_lengths))
    outputs_all, grads_all = stacked
    return (outputs_all.reshape(TOKENS, D), grads_all.reshape(TOKENS, D), totals[0], totals[1], totals[2], totals[3], totals[4], totals[5], totals[6], totals[7], totals[8])
```

```python
import math

import jax
import jax.numpy as jnp
from jax import lax
from jax.sharding import PartitionSpec as P

HD = 64
MAXLEN = 512

eps_norm = 1e-05
rope_base = 500000.0

BF = jnp.bfloat16
F32 = jnp.float32


def layout(lengths, token_index):
    seq_ends = jnp.cumsum(lengths, axis=1)
    passed = (token_index[None, :, None] >= seq_ends[:, None, :]).astype(jnp.int32)
    segment = jnp.sum(passed, axis=2)
    seq_start = jnp.sum(passed * lengths[:, None, :], axis=2)
    return segment, token_index[None, :] - seq_start


def rope_tables(position):
    half_width = HD // 2
    frequency = rope_base ** (-jnp.arange(half_width, dtype=F32) / half_width)
    angles = position.astype(F32)[:, None] * frequency[None, :]
    return jnp.cos(angles), jnp.sin(angles)


def rotate(vectors, cosine_table, sine_table, direction):
    half_width = HD // 2
    first_half = vectors[..., :half_width]
    second = vectors[..., half_width:]
    cos_rows = cosine_table[:, None, :]
    sin_rows = direction * sine_table[:, None, :]
    return jnp.concatenate(
        [first_half * cos_rows - second * sin_rows, second * cos_rows + first_half * sin_rows],
        axis=-1,
    )


def norm_forward(rows_wide):
    inv_rms = lax.rsqrt(jnp.mean(rows_wide * rows_wide, axis=-1, keepdims=True) + eps_norm)
    return rows_wide * inv_rms, inv_rms


def norm_backward(delta_rows, unit_rows, inv_rms, gain_wide):
    scaled = gain_wide[None, :] * delta_rows
    gain_term = jnp.sum(delta_rows * unit_rows, axis=0)
    back_term = inv_rms * (
        scaled - unit_rows * jnp.mean(scaled * unit_rows, axis=-1, keepdims=True)
    )
    return gain_term, back_term


def dot(a, b):
    return jnp.dot(a, b, preferred_element_type=F32)


def dot_t(a, b):
    return lax.dot_general(a, b, (((0,), (0,)), ((), ())), preferred_element_type=F32)


def dot_bt(a, b):
    return lax.dot_general(a, b, (((1,), (1,)), ((), ())), preferred_element_type=F32)


def after(value, *deps):
    return lax.optimization_barrier((value,) + deps)[0]


def body(
    block_input,
    seq_lengths,
    attn_gain,
    w_query,
    w_key,
    w_value,
    w_output,
    mlp_gain,
    w_gate,
    w_up,
    w_down,
    cotangent,
):
    rows, width = block_input.shape
    n_fsdp, n_ctx, n_ten = (lax.axis_size(a) for a in ("fsdp", "ctx", "tensor"))
    heads_local = w_query.shape[1] // HD
    kv_local = w_key.shape[1] // HD
    tp = math.gcd(n_fsdp, kv_local)
    n_out = n_fsdp // tp
    hq, hk = heads_local // tp, kv_local // tp
    share = hq // hk
    ff_part = w_gate.shape[1] // tp
    d_blk = w_query.shape[0]
    score_scale = 1.0 / math.sqrt(HD)
    i = lax.axis_index("fsdp")
    j = i % tp
    z = lax.axis_index("ctx")
    outer_groups = [[o * tp + jj for o in range(n_out)] for jj in range(tp)]
    bits = []
    b = tp // 2
    while b:
        bits.append(b)
        b //= 2

    def swap(v, r):
        return lax.ppermute(v, "fsdp", [(s, s ^ r) for s in range(n_fsdp)])

    def shift(v, s, first=0, last=None):
        last = n_ctx if last is None else last
        return lax.ppermute(
            v, "ctx", [(k, k + s) for k in range(first, last) if 0 <= k + s < n_ctx]
        )

    def gather_rows(v):
        for bit in bits:
            v = jnp.concatenate([v, swap(v, bit)], axis=0)
        return v

    def ten_sum(acc):
        low = acc.astype(BF)
        if n_ten == 1:
            return low.astype(F32)
        if n_ten == 2:
            return low.astype(F32) + lax.ppermute(low, "tensor", [(0, 1), (1, 0)]).astype(F32)
        return lax.psum(low, "tensor").astype(F32)

    def reduce_rows(pairs, mult):
        total = tp * rows
        half = total // 2 if tp > 1 else total
        own = sum(mult(a[:half], w) for a, w in pairs)
        if tp > 1:
            send = sum(mult(a[half:], w) for a, w in pairs).astype(BF)
            own = own + swap(send, bits[-1]).astype(F32)
        for bit in reversed(bits[:-1]):
            half //= 2
            own = own[:half] + swap(own[half:].astype(BF), bit).astype(F32)
        return ten_sum(own)

    def place(buffer, value, start, axis):
        starts = [0] * buffer.ndim
        starts[axis] = start
        return lax.dynamic_update_slice(buffer, value, starts)

    def fetch(piece, axis, dep=None):
        hold = (lambda v: v) if dep is None else (lambda v: after(v, *dep))
        got = [(piece(j), j)]
        direct = list(range(1, tp))
        if tp == 4 and n_ctx % 2 == 0:
            direct = [1]
            odd = z % 2
            perm = [
                (s * n_ctx + k, (s ^ (2 + k % 2)) * n_ctx + k)
                for s in range(n_fsdp)
                for k in range(n_ctx)
            ]
            first = lax.ppermute(hold(piece(j ^ (2 + odd))), ("fsdp", "ctx"), perm)
            second = lax.ppermute(first, "ctx", [(k, k ^ 1) for k in range(n_ctx)])
            got += [(first, j ^ (2 + odd)), (second, j ^ (3 - odd))]
        for r in direct:
            got.append((swap(hold(piece(j ^ r)), r), j ^ r))
        size = got[0][0].shape[axis]
        shape = list(got[0][0].shape)
        shape[axis] = tp * size
        full = jnp.zeros(shape, BF)
        for value, k in got:
            full = place(full, value, k * size, axis)
        if n_out > 1:
            full = lax.all_gather(full, "fsdp", axis=axis, tiled=True, axis_index_groups=outer_groups)
        return full, got[1][0] if tp > 1 else full

    def cols(w, k, size):
        return lax.dynamic_slice_in_dim(w, k * size, size, axis=1)

    def take_rows(w, k, size):
        return lax.dynamic_slice_in_dim(w, k * size, size, axis=0)

    gains = jnp.stack([attn_gain, mlp_gain])
    gain_all = place(jnp.zeros((2, tp * d_blk), BF), gains, j * d_blk, 1)
    for r in range(1, tp):
        gain_all = place(gain_all, swap(gains, r), (j ^ r) * d_blk, 1)
    if n_out > 1:
        gain_all = lax.all_gather(gain_all, "fsdp", axis=1, tiled=True, axis_index_groups=outer_groups)
    gain_one = gain_all[0].astype(F32)
    gain_two = gain_all[1].astype(F32)
    lengths = gather_rows(seq_lengths)

    input_wide = block_input.astype(F32)
    unit_one, rstd_one = norm_forward(input_wide)
    own_normed = (unit_one * gain_one[None, :]).astype(BF)
    normed_one = gather_rows(own_normed)
    qkv_full, _ = fetch(
        lambda k: jnp.concatenate(
            [cols(w_query, k, hq * HD), cols(w_key, k, hk * HD), cols(w_value, k, hk * HD)], axis=1
        ),
        0,
    )
    out_full, out_dep = fetch(lambda k: take_rows(w_output, k, hq * HD), 1, (normed_one,))
    gate_full, gate_dep = fetch(lambda k: cols(w_gate, k, ff_part), 0, (normed_one, out_dep))
    up_full, up_dep = fetch(lambda k: cols(w_up, k, ff_part), 0, (gate_dep,))

    qkv = dot(normed_one, qkv_full)
    local_index = z * rows + jnp.arange(rows, dtype=jnp.int32)
    q_seg, q_pos = layout(lengths, local_index)
    cosine_table, sine_table = rope_tables(q_pos.reshape(tp * rows))
    q_cols, k_cols = hq * HD, hk * HD
    query_rot = rotate(
        qkv[:, :q_cols].reshape(tp * rows, hq, HD), cosine_table, sine_table, 1.0
    ).astype(BF)
    key_rot = rotate(
        qkv[:, q_cols : q_cols + k_cols].reshape(tp * rows, hk, HD), cosine_table, sine_table, 1.0
    ).astype(BF)
    value_rows = qkv[:, q_cols + k_cols :].astype(BF)

    reach = min(-(-(MAXLEN - 1) // rows), n_ctx - 1)
    kv_own = jnp.concatenate([key_rot.reshape(tp * rows, k_cols), value_rows], axis=1)
    kv_blocks = [kv_own] + [shift(kv_own, s) for s in range(1, reach + 1)]
    kv_all = jnp.concatenate(
        [v.reshape(tp, 1, rows, 2, hk, HD) for v in kv_blocks], axis=1
    ).reshape(tp, (reach + 1) * rows, 2, hk, HD)
    key_index = jnp.concatenate(
        [(z - s) * rows + jnp.arange(rows, dtype=jnp.int32) for s in range(reach + 1)]
    )
    k_seg, _ = layout(lengths, key_index)
    allowed = (
        (q_seg[:, :, None] == k_seg[:, None, :])
        & (key_index[None, None, :] <= local_index[None, :, None])
        & (key_index[None, None, :] >= 0)
    )[:, None, None]
    q_h = query_rot.reshape(tp, rows, hk, share, HD).transpose(0, 2, 3, 1, 4)
    k_h = kv_all[:, :, 0].transpose(0, 2, 1, 3)
    v_h = kv_all[:, :, 1].transpose(0, 2, 1, 3)

    scores = jnp.einsum("bgrtd,bgsd->bgrts", q_h, k_h, preferred_element_type=F32) * score_scale
    masked = jnp.where(allowed, scores, -1e30)
    row_max = jnp.max(masked, axis=-1, keepdims=True)
    exp_total = jnp.sum(jnp.where(allowed, jnp.exp(masked - row_max), 0.0), axis=-1, keepdims=True)
    log_total = row_max + jnp.log(exp_total)
    prob = jnp.where(allowed, jnp.exp(masked - log_total), 0.0)
    prob_low = prob.astype(BF)
    attended = jnp.einsum("bgrts,bgsd->bgrtd", prob_low, v_h, preferred_element_type=F32).astype(BF)
    attended_rows = attended.transpose(0, 3, 1, 2, 4).reshape(tp * rows, hq * HD)
    residual = input_wide + reduce_rows([(attended_rows, out_full)], dot)

    unit_two, rstd_two = norm_forward(residual)
    own_normed_two = (unit_two * gain_two[None, :]).astype(BF)
    normed_two = gather_rows(own_normed_two)
    down_full, down_dep = fetch(lambda k: take_rows(w_down, k, ff_part), 1, (up_dep,))
    cot_all = gather_rows(after(cotangent, down_dep))
    gate_pre = dot(normed_two, gate_full)
    up_pre = dot(normed_two, up_full)
    sigmoid_gate = jax.nn.sigmoid(gate_pre)
    silu_gate = gate_pre * sigmoid_gate
    activation = (silu_gate * up_pre).astype(BF)
    act_delta = dot_bt(cot_all, down_full)
    silu_slope = sigmoid_gate * (1.0 + gate_pre * (1.0 - sigmoid_gate))
    gate_delta = (act_delta * up_pre * silu_slope).astype(BF)
    up_delta = (act_delta * silu_gate).astype(BF)

    def ctx_sum(unit):
        right = left = None
        for s in range(1, n_ctx):
            out_r = unit(jnp.clip(n_ctx - s + z, 0, n_ctx - 1))
            out_l = unit(jnp.clip(s - n_ctx + z, 0, n_ctx - 1))
            if right is not None:
                out_r = (out_r.astype(F32) + right.astype(F32)).astype(BF)
                out_l = (out_l.astype(F32) + left.astype(F32)).astype(BF)
            right = shift(out_r, 1, 0, s)
            left = shift(out_l, -1, n_ctx - s, n_ctx)
        own = unit(z)
        if right is None:
            return own
        return (own.astype(F32) + right.astype(F32) + left.astype(F32)).astype(BF)

    def ctx_blocks(v):
        out = [(z, v.astype(F32))]
        right, left = [v], [v]
        for s in range(1, n_ctx):
            right.append(shift(right[-1], 1, s - 1, n_ctx))
            left.append(shift(left[-1], -1, 0, n_ctx - s + 1))
        for s in range(1, n_ctx):
            out.append(((z - s) % n_ctx, right[s].astype(F32) + left[n_ctx - s].astype(F32)))
        return out

    def exchange(piece):
        return [(j, piece(j))] + [(j ^ r, swap(piece(j ^ r), r)) for r in range(1, tp)]

    def finish_rows(part, widths):
        b = d_blk // n_ctx
        c = part.shape[1]
        view = part.reshape(n_fsdp, n_ctx, b, c)
        own = ctx_sum(lambda t: lax.dynamic_slice_in_dim(view, t, 1, axis=1)[:, 0])
        if n_out > 1:
            own = lax.psum_scatter(
                own.reshape(n_out, tp, b, c), "fsdp", scatter_dimension=0, axis_index_groups=outer_groups
            )
        got = exchange(lambda k: lax.dynamic_slice_in_dim(own, k, 1, axis=0)[0])
        mine = jnp.zeros((b, tp * c), BF)
        base = low = 0
        for w in widths:
            for k, value in got:
                mine = lax.dynamic_update_slice(mine, value[:, low : low + w], (0, base + k * w))
            base, low = base + tp * w, low + w
        full = jnp.zeros((n_ctx, b, tp * c), F32)
        for k, value in ctx_blocks(mine):
            full = lax.dynamic_update_slice(full, value[None], (k, 0, 0))
        return full.reshape(d_blk, tp * c)

    def finish_cols(part):
        b = part.shape[0] // n_ctx
        own = ctx_sum(lambda t: take_rows(part, t, b))
        if n_out > 1:
            own = lax.psum_scatter(
                own.reshape(b, n_out, tp * d_blk), "fsdp", scatter_dimension=1, axis_index_groups=outer_groups
            )
        got = exchange(lambda k: cols(own, k, d_blk))
        mine = jnp.zeros((tp, b, d_blk), BF)
        for k, value in got:
            mine = lax.dynamic_update_slice(mine, value[None], (k, 0, 0))
        full = jnp.zeros((tp, n_ctx, b, d_blk), F32)
        for k, value in ctx_blocks(mine):
            full = lax.dynamic_update_slice(full, value[:, None], (0, k, 0, 0))
        return full.reshape(tp * n_ctx * b, d_blk)

    down_out = finish_cols(dot_t(activation, cot_all).astype(BF))
    gate_out = finish_rows(dot_t(normed_two, gate_delta).astype(BF), (ff_part,))
    up_out = finish_rows(dot_t(normed_two, up_delta).astype(BF), (ff_part,))

    normed_two_delta = reduce_rows([(gate_delta, gate_full), (up_delta, up_full)], dot_bt)
    gain_two_term, residual_back = norm_backward(normed_two_delta, unit_two, rstd_two, gain_two)
    residual_delta = cotangent.astype(F32) + residual_back
    residual_low = gather_rows(residual_delta.astype(BF))
    block_output = (residual + reduce_rows([(activation, down_full)], dot)).astype(BF)

    output_out = finish_cols(dot_t(attended_rows, residual_low).astype(BF))
    attended_delta = dot_bt(residual_low, out_full).astype(BF)
    delta_h = attended_delta.reshape(tp, rows, hk, share, HD).transpose(0, 2, 3, 1, 4)
    inner_rows = jnp.sum(attended.astype(F32) * delta_h.astype(F32), axis=-1, keepdims=True)
    prob_delta = jnp.einsum("bgrtd,bgsd->bgrts", delta_h, v_h, preferred_element_type=F32)
    score_delta = (prob * (prob_delta - inner_rows) * score_scale).astype(BF)
    query_back = jnp.einsum("bgrts,bgsd->bgrtd", score_delta, k_h, preferred_element_type=F32)
    key_back = jnp.einsum("bgrts,bgrtd->bgsd", score_delta, q_h, preferred_element_type=F32)
    value_back = jnp.einsum("bgrts,bgrtd->bgsd", prob_low, delta_h, preferred_element_type=F32)

    def to_blocks(v):
        v = v.transpose(0, 2, 1, 3).reshape(tp, reach + 1, rows, k_cols)
        return [v[:, s].reshape(tp * rows, k_cols) for s in range(reach + 1)]

    kv_back = [
        jnp.concatenate([kb, vb], axis=1) for kb, vb in zip(to_blocks(key_back), to_blocks(value_back))
    ]
    kv_sum = kv_back[0]
    for s in range(1, reach + 1):
        kv_sum = kv_sum + shift(kv_back[s].astype(BF), -s).astype(F32)
    query_delta = rotate(
        query_back.transpose(0, 3, 1, 2, 4).reshape(tp * rows, hq, HD), cosine_table, sine_table, -1.0
    ).reshape(tp * rows, q_cols)
    key_delta = rotate(
        kv_sum[:, :k_cols].reshape(tp * rows, hk, HD), cosine_table, sine_table, -1.0
    ).reshape(tp * rows, k_cols)
    qkv_delta = jnp.concatenate([query_delta, key_delta, kv_sum[:, k_cols:]], axis=1).astype(BF)
    qkv_out = finish_rows(dot_t(normed_one, qkv_delta).astype(BF), (q_cols, k_cols, k_cols))
    normed_one_delta = reduce_rows([(qkv_delta, qkv_full)], dot_bt)
    gain_one_term, input_back = norm_backward(normed_one_delta, unit_one, rstd_one, gain_one)
    input_grad = residual_delta + input_back

    terms = jnp.stack([gain_one_term, gain_two_term])
    if n_out > 1:
        terms = lax.psum_scatter(
            terms.reshape(2, n_out, tp * d_blk), "fsdp", scatter_dimension=1, axis_index_groups=outer_groups
        )
    got = exchange(lambda k: cols(terms, k, d_blk))
    gain_sum = sum(value for _, value in got)
    table = place(jnp.zeros((n_ctx,) + gain_sum.shape, F32), gain_sum[None], z, 0)
    for s in range(1, n_ctx):
        other = lax.ppermute(gain_sum, "ctx", [(k, (k + s) % n_ctx) for k in range(n_ctx)])
        table = place(table, other[None], (z - s) % n_ctx, 0)
    gain_grads = jnp.sum(table, axis=0)

    q_all, k_all = tp * q_cols, tp * k_cols
    return (
        block_output,
        input_grad,
        gain_grads[0],
        qkv_out[:, :q_all],
        qkv_out[:, q_all : q_all + k_all],
        qkv_out[:, q_all + k_all :],
        output_out,
        gain_grads[1],
        gate_out,
        up_out,
        down_out,
    )


def solution(mesh):
    in_specs = (
        P(("fsdp", "ctx"), None),
        P("fsdp", None),
        P("fsdp"),
        P("fsdp", "tensor"),
        P("fsdp", "tensor"),
        P("fsdp", "tensor"),
        P("tensor", "fsdp"),
        P("fsdp"),
        P("fsdp", "tensor"),
        P("fsdp", "tensor"),
        P("tensor", "fsdp"),
        P(("fsdp", "ctx"), None),
    )
    out_specs = (
        P(("fsdp", "ctx"), None),
        P(("fsdp", "ctx"), None),
        P("fsdp"),
        P("fsdp", "tensor"),
        P("fsdp", "tensor"),
        P("fsdp", "tensor"),
        P("tensor", "fsdp"),
        P("fsdp"),
        P("fsdp", "tensor"),
        P("fsdp", "tensor"),
        P("tensor", "fsdp"),
    )
    return jax.shard_map(body, mesh=mesh, in_specs=in_specs, out_specs=out_specs, check_vma=False)
```

```python
import math

import jax
import jax.numpy as jnp
from jax import lax
from jax.sharding import PartitionSpec as P

HD = 64
MAXLEN = 512

eps_norm = 1e-05
rope_base = 500000.0

BF = jnp.bfloat16
F32 = jnp.float32


def layout(lengths, token_index):
    seq_ends = jnp.cumsum(lengths, axis=1)
    passed = (token_index[None, :, None] >= seq_ends[:, None, :]).astype(jnp.int32)
    segment = jnp.sum(passed, axis=2)
    seq_start = jnp.sum(passed * lengths[:, None, :], axis=2)
    return segment, token_index[None, :] - seq_start


def rope_tables(position):
    half_width = HD // 2
    frequency = rope_base ** (-jnp.arange(half_width, dtype=F32) / half_width)
    angles = position.astype(F32)[:, None] * frequency[None, :]
    return jnp.cos(angles), jnp.sin(angles)


def rotate(vectors, cosine_table, sine_table, direction):
    half_width = HD // 2
    first_half = vectors[..., :half_width]
    second = vectors[..., half_width:]
    cos_rows = cosine_table[:, None, :]
    sin_rows = direction * sine_table[:, None, :]
    return jnp.concatenate(
        [first_half * cos_rows - second * sin_rows, second * cos_rows + first_half * sin_rows],
        axis=-1,
    )


def norm_forward(rows_wide):
    inv_rms = lax.rsqrt(jnp.mean(rows_wide * rows_wide, axis=-1, keepdims=True) + eps_norm)
    return rows_wide * inv_rms, inv_rms


def norm_backward(delta_rows, unit_rows, inv_rms, gain_wide):
    scaled = gain_wide[None, :] * delta_rows
    gain_term = jnp.sum(delta_rows * unit_rows, axis=0)
    back_term = inv_rms * (
        scaled - unit_rows * jnp.mean(scaled * unit_rows, axis=-1, keepdims=True)
    )
    return gain_term, back_term


def dot(a, b):
    return jnp.dot(a, b, preferred_element_type=F32)


def dot_t(a, b):
    return lax.dot_general(a, b, (((0,), (0,)), ((), ())), preferred_element_type=F32)


def dot_bt(a, b):
    return lax.dot_general(a, b, (((1,), (1,)), ((), ())), preferred_element_type=F32)


def after(value, *deps):
    return lax.optimization_barrier((value,) + deps)[0] if deps else value


def body(
    block_input,
    seq_lengths,
    attn_gain,
    w_query,
    w_key,
    w_value,
    w_output,
    mlp_gain,
    w_gate,
    w_up,
    w_down,
    cotangent,
):
    rows, width = block_input.shape
    n_fsdp, n_ctx, n_ten = (lax.axis_size(a) for a in ("fsdp", "ctx", "tensor"))
    heads_local = w_query.shape[1] // HD
    kv_local = w_key.shape[1] // HD
    tp = math.gcd(n_fsdp, kv_local)
    n_out = n_fsdp // tp
    hq, hk = heads_local // tp, kv_local // tp
    share = hq // hk
    ff_part = w_gate.shape[1] // tp
    d_blk = w_query.shape[0]
    score_scale = 1.0 / math.sqrt(HD)
    i = lax.axis_index("fsdp")
    j = i % tp
    z = lax.axis_index("ctx")
    outer_groups = [[o * tp + jj for o in range(n_out)] for jj in range(tp)]
    bits = []
    b = tp // 2
    while b:
        bits.append(b)
        b //= 2

    def swap(v, r):
        return lax.ppermute(v, "fsdp", [(s, s ^ r) for s in range(n_fsdp)])

    def shift(v, s, first=0, last=None):
        last = n_ctx if last is None else last
        return lax.ppermute(
            v, "ctx", [(k, k + s) for k in range(first, last) if 0 <= k + s < n_ctx]
        )

    def gather_rows(v):
        return gather_steps(v)[0]

    def gather_steps(v):
        landed = []
        for bit in bits:
            landed.append(swap(v, bit))
            v = jnp.concatenate([v, landed[-1]], axis=0)
        return v, landed

    def ten_sum(acc):
        low = acc.astype(BF)
        if n_ten == 1:
            return low.astype(F32)
        if n_ten == 2:
            return low.astype(F32) + lax.ppermute(low, "tensor", [(0, 1), (1, 0)]).astype(F32)
        return lax.psum(low, "tensor").astype(F32)

    def reduce_rows(pairs, mult):
        return reduce_steps(pairs, mult)[0]

    def reduce_steps(pairs, mult):
        total = tp * rows
        half = total // 2 if tp > 1 else total
        landed = []
        own = sum(mult(a[:half], w) for a, w in pairs)
        if tp > 1:
            send = sum(mult(a[half:], w) for a, w in pairs).astype(BF)
            landed.append(swap(send, bits[-1]))
            own = own + landed[-1].astype(F32)
        for bit in reversed(bits[:-1]):
            half //= 2
            landed.append(swap(own[half:].astype(BF), bit))
            own = own[:half] + landed[-1].astype(F32)
        return ten_sum(own), landed

    def place(buffer, value, start, axis):
        starts = [0] * buffer.ndim
        starts[axis] = start
        return lax.dynamic_update_slice(buffer, value, starts)

    def fetch(piece, axis, first_dep=(), second_dep=()):
        got = [(piece(j), j)]
        direct = list(range(1, tp))
        landed = ()
        if tp == 4 and n_ctx % 2 == 0:
            direct = [1]
            odd = z % 2
            perm = [
                (s * n_ctx + k, (s ^ (2 + k % 2)) * n_ctx + k)
                for s in range(n_fsdp)
                for k in range(n_ctx)
            ]
            first = lax.ppermute(after(piece(j ^ (2 + odd)), *first_dep), ("fsdp", "ctx"), perm)
            second = lax.ppermute(after(first, *second_dep), "ctx", [(k, k ^ 1) for k in range(n_ctx)])
            got += [(first, j ^ (2 + odd)), (second, j ^ (3 - odd))]
            landed = (first,)
        for r in direct:
            got.append((swap(after(piece(j ^ r), *first_dep), r), j ^ r))
        size = got[0][0].shape[axis]
        shape = list(got[0][0].shape)
        shape[axis] = tp * size
        full = jnp.zeros(shape, BF)
        for value, k in got:
            full = place(full, value, k * size, axis)
        if n_out > 1:
            full = lax.all_gather(full, "fsdp", axis=axis, tiled=True, axis_index_groups=outer_groups)
        return full, landed

    def cols(w, k, size):
        return lax.dynamic_slice_in_dim(w, k * size, size, axis=1)

    def take_rows(w, k, size):
        return lax.dynamic_slice_in_dim(w, k * size, size, axis=0)

    gains = jnp.stack([attn_gain, mlp_gain])
    gain_all = place(jnp.zeros((2, tp * d_blk), BF), gains, j * d_blk, 1)
    for r in range(1, tp):
        gain_all = place(gain_all, swap(gains, r), (j ^ r) * d_blk, 1)
    if n_out > 1:
        gain_all = lax.all_gather(gain_all, "fsdp", axis=1, tiled=True, axis_index_groups=outer_groups)
    gain_one = gain_all[0].astype(F32)
    gain_two = gain_all[1].astype(F32)
    lengths = gather_rows(seq_lengths)

    input_wide = block_input.astype(F32)
    unit_one, rstd_one = norm_forward(input_wide)
    own_normed = (unit_one * gain_one[None, :]).astype(BF)
    normed_one, normed_landed = gather_steps(own_normed)
    qkv_full, _ = fetch(
        lambda k: jnp.concatenate(
            [cols(w_query, k, hq * HD), cols(w_key, k, hk * HD), cols(w_value, k, hk * HD)], axis=1
        ),
        0,
    )
    out_full, _ = fetch(
        lambda k: take_rows(w_output, k, hq * HD), 1, normed_landed[:1], normed_landed[-1:]
    )

    qkv = dot(normed_one, qkv_full)
    local_index = z * rows + jnp.arange(rows, dtype=jnp.int32)
    q_seg, q_pos = layout(lengths, local_index)
    cosine_table, sine_table = rope_tables(q_pos.reshape(tp * rows))
    q_cols, k_cols = hq * HD, hk * HD
    query_rot = rotate(
        qkv[:, :q_cols].reshape(tp * rows, hq, HD), cosine_table, sine_table, 1.0
    ).astype(BF)
    key_rot = rotate(
        qkv[:, q_cols : q_cols + k_cols].reshape(tp * rows, hk, HD), cosine_table, sine_table, 1.0
    ).astype(BF)
    value_rows = qkv[:, q_cols + k_cols :].astype(BF)

    reach = min(-(-(MAXLEN - 1) // rows), n_ctx - 1)
    kv_own = jnp.concatenate([key_rot.reshape(tp * rows, k_cols), value_rows], axis=1)
    kv_blocks = [kv_own] + [shift(kv_own, s) for s in range(1, reach + 1)]
    kv_dep = tuple(kv_blocks[1:])
    gate_full, _ = fetch(lambda k: cols(w_gate, k, ff_part), 0, normed_landed[:1], kv_dep)
    kv_all = jnp.concatenate(
        [v.reshape(tp, 1, rows, 2, hk, HD) for v in kv_blocks], axis=1
    ).reshape(tp, (reach + 1) * rows, 2, hk, HD)
    key_index = jnp.concatenate(
        [(z - s) * rows + jnp.arange(rows, dtype=jnp.int32) for s in range(reach + 1)]
    )
    k_seg, _ = layout(lengths, key_index)
    allowed = (
        (q_seg[:, :, None] == k_seg[:, None, :])
        & (key_index[None, None, :] <= local_index[None, :, None])
        & (key_index[None, None, :] >= 0)
    )[:, None, None]
    q_h = query_rot.reshape(tp, rows, hk, share, HD).transpose(0, 2, 3, 1, 4)
    k_h = kv_all[:, :, 0].transpose(0, 2, 1, 3)
    v_h = kv_all[:, :, 1].transpose(0, 2, 1, 3)

    scores = jnp.einsum("bgrtd,bgsd->bgrts", q_h, k_h, preferred_element_type=F32) * score_scale
    masked = jnp.where(allowed, scores, -1e30)
    row_max = jnp.max(masked, axis=-1, keepdims=True)
    exp_total = jnp.sum(jnp.where(allowed, jnp.exp(masked - row_max), 0.0), axis=-1, keepdims=True)
    log_total = row_max + jnp.log(exp_total)
    prob = jnp.where(allowed, jnp.exp(masked - log_total), 0.0)
    prob_low = prob.astype(BF)
    attended = jnp.einsum("bgrts,bgsd->bgrtd", prob_low, v_h, preferred_element_type=F32).astype(BF)
    attended_rows = attended.transpose(0, 3, 1, 2, 4).reshape(tp * rows, hq * HD)
    attn_sum, attn_landed = reduce_steps([(attended_rows, out_full)], dot)
    up_full, _ = fetch(lambda k: cols(w_up, k, ff_part), 0, kv_dep, attn_landed[:1])
    residual = input_wide + attn_sum

    unit_two, rstd_two = norm_forward(residual)
    own_normed_two = (unit_two * gain_two[None, :]).astype(BF)
    normed_two, two_landed = gather_steps(own_normed_two)
    cot_all = gather_rows(after(cotangent, *attn_landed[-1:]))
    half = ff_part // 2
    down_low, _ = fetch(
        lambda k: lax.dynamic_slice_in_dim(w_down, k * ff_part, half, axis=0),
        1, attn_landed[-1:], (residual,),
    )
    down_high, _ = fetch(
        lambda k: lax.dynamic_slice_in_dim(w_down, k * ff_part + half, half, axis=0),
        1, two_landed[:1], two_landed[-1:],
    )
    down_full = jnp.concatenate([down_low, down_high], axis=0)
    gate_pre = dot(normed_two, gate_full)
    up_pre = dot(normed_two, up_full)
    sigmoid_gate = jax.nn.sigmoid(gate_pre)
    silu_gate = gate_pre * sigmoid_gate
    activation = (silu_gate * up_pre).astype(BF)
    act_delta = dot_bt(cot_all, down_full)
    silu_slope = sigmoid_gate * (1.0 + gate_pre * (1.0 - sigmoid_gate))
    gate_delta = (act_delta * up_pre * silu_slope).astype(BF)
    up_delta = (act_delta * silu_gate).astype(BF)

    mid = n_ctx // 2

    def ctx_sum(part):
        acc = part
        for h in range(mid - 1):
            come = lax.ppermute(acc, "ctx", [(h, h + 1), (n_ctx - 1 - h, n_ctx - 2 - h)])
            acc = (part.astype(F32) + come.astype(F32)).astype(BF)
        come = lax.ppermute(acc, "ctx", [(mid - 1, mid), (mid, mid - 1)])
        return (acc.astype(F32) + come.astype(F32)).astype(BF)

    def ctx_spread(value):
        for h in reversed(range(mid - 1)):
            come = lax.ppermute(value, "ctx", [(h + 1, h), (n_ctx - 2 - h, n_ctx - 1 - h)])
            value = jnp.where((z == h) | (z == n_ctx - 1 - h), come, value)
        return value

    def exchange(piece, planes=None):
        planes = range(n_ctx) if planes is None else planes
        out = [(j, piece(j))]
        for r in range(1, tp):
            perm = [(s * n_ctx + k, (s ^ r) * n_ctx + k) for s in range(n_fsdp) for k in planes]
            out.append((j ^ r, lax.ppermute(piece(j ^ r), ("fsdp", "ctx"), perm)))
        return out

    def finish_rows(view, widths):
        _, b, c = view.shape
        own = ctx_sum(view)
        if n_out > 1:
            own = lax.psum_scatter(
                own.reshape(n_out, tp, b, c), "fsdp", scatter_dimension=0, axis_index_groups=outer_groups
            )
        got = exchange(lambda k: lax.dynamic_slice_in_dim(own, k, 1, axis=0)[0], (mid - 1, mid))
        mine = jnp.zeros((b, tp * c), BF)
        base = low = 0
        for w in widths:
            for k, value in got:
                mine = lax.dynamic_update_slice(mine, value[:, low : low + w], (0, base + k * w))
            base, low = base + tp * w, low + w
        return ctx_spread(mine)

    def finish_cols(part):
        b = part.shape[0]
        own = ctx_sum(part)
        if n_out > 1:
            own = lax.psum_scatter(
                own.reshape(b, n_out, tp * d_blk), "fsdp", scatter_dimension=1, axis_index_groups=outer_groups
            )
        got = exchange(lambda k: cols(own, k, d_blk), (mid - 1, mid))
        mine = jnp.zeros((tp, b, d_blk), BF)
        for k, value in got:
            mine = lax.dynamic_update_slice(mine, value[None], (k, 0, 0))
        return ctx_spread(mine)

    def grad_cols(left, right, chunks):
        b = left.shape[1] // chunks
        done = [
            finish_cols(dot_t(left[:, n * b : (n + 1) * b], right).astype(BF)) for n in range(chunks)
        ]
        full = jnp.stack([v.astype(F32) for v in done], axis=1)
        return full.reshape(tp * chunks * b, d_blk)

    def grad_rows(left, right, widths, chunks):
        b = d_blk // chunks
        part = dot_t(left, right).astype(BF).reshape(n_fsdp, chunks, b, right.shape[1])
        done = [finish_rows(part[:, n], widths) for n in range(chunks)]
        return jnp.concatenate([v.astype(F32) for v in done], axis=0)

    down_out = grad_cols(activation, cot_all, 2)
    up_out = grad_rows(normed_two, up_delta, (ff_part,), 2)
    gate_out = grad_rows(normed_two, gate_delta, (ff_part,), 2)

    normed_two_delta = reduce_rows([(gate_delta, gate_full), (up_delta, up_full)], dot_bt)
    gain_two_term, residual_back = norm_backward(normed_two_delta, unit_two, rstd_two, gain_two)
    residual_delta = cotangent.astype(F32) + residual_back
    residual_low = gather_rows(residual_delta.astype(BF))

    output_out = grad_cols(attended_rows, residual_low, 1)
    attended_delta = dot_bt(residual_low, out_full).astype(BF)
    delta_h = attended_delta.reshape(tp, rows, hk, share, HD).transpose(0, 2, 3, 1, 4)
    inner_rows = jnp.sum(attended.astype(F32) * delta_h.astype(F32), axis=-1, keepdims=True)
    prob_delta = jnp.einsum("bgrtd,bgsd->bgrts", delta_h, v_h, preferred_element_type=F32)
    score_delta = (prob * (prob_delta - inner_rows) * score_scale).astype(BF)
    query_back = jnp.einsum("bgrts,bgsd->bgrtd", score_delta, k_h, preferred_element_type=F32)
    key_back = jnp.einsum("bgrts,bgrtd->bgsd", score_delta, q_h, preferred_element_type=F32)
    value_back = jnp.einsum("bgrts,bgrtd->bgsd", prob_low, delta_h, preferred_element_type=F32)

    def to_blocks(v):
        v = v.transpose(0, 2, 1, 3).reshape(tp, reach + 1, rows, k_cols)
        return [v[:, s].reshape(tp * rows, k_cols) for s in range(reach + 1)]

    kv_back = [
        jnp.concatenate([kb, vb], axis=1) for kb, vb in zip(to_blocks(key_back), to_blocks(value_back))
    ]
    kv_sum = kv_back[0]
    for s in range(1, reach + 1):
        kv_sum = kv_sum + shift(kv_back[s].astype(BF), -s).astype(F32)
    query_delta = rotate(
        query_back.transpose(0, 3, 1, 2, 4).reshape(tp * rows, hq, HD), cosine_table, sine_table, -1.0
    ).reshape(tp * rows, q_cols)
    key_delta = rotate(
        kv_sum[:, :k_cols].reshape(tp * rows, hk, HD), cosine_table, sine_table, -1.0
    ).reshape(tp * rows, k_cols)
    qkv_delta = jnp.concatenate([query_delta, key_delta, kv_sum[:, k_cols:]], axis=1).astype(BF)
    qkv_out = grad_rows(normed_one, qkv_delta, (q_cols, k_cols, k_cols), 1)
    late = after(activation, attended_delta)
    block_output = (residual + reduce_rows([(late, down_full)], dot)).astype(BF)
    normed_one_delta = reduce_rows([(qkv_delta, qkv_full)], dot_bt)
    gain_one_term, input_back = norm_backward(normed_one_delta, unit_one, rstd_one, gain_one)
    input_grad = residual_delta + input_back

    terms = jnp.stack([gain_one_term, gain_two_term])
    if n_out > 1:
        terms = lax.psum_scatter(
            terms.reshape(2, n_out, tp * d_blk), "fsdp", scatter_dimension=1, axis_index_groups=outer_groups
        )
    got = exchange(lambda k: cols(terms, k, d_blk))
    gain_sum = sum(value for _, value in got)
    step = 1
    while step < n_ctx:
        gain_sum = gain_sum + lax.ppermute(gain_sum, "ctx", [(k, k ^ step) for k in range(n_ctx)])
        step *= 2
    gain_grads = gain_sum

    q_all, k_all = tp * q_cols, tp * k_cols
    return (
        block_output,
        input_grad,
        gain_grads[0],
        qkv_out[:, :q_all],
        qkv_out[:, q_all : q_all + k_all],
        qkv_out[:, q_all + k_all :],
        output_out,
        gain_grads[1],
        gate_out,
        up_out,
        down_out,
    )


def solution(mesh):
    in_specs = (
        P(("fsdp", "ctx"), None),
        P("fsdp", None),
        P("fsdp"),
        P("fsdp", "tensor"),
        P("fsdp", "tensor"),
        P("fsdp", "tensor"),
        P("tensor", "fsdp"),
        P("fsdp"),
        P("fsdp", "tensor"),
        P("fsdp", "tensor"),
        P("tensor", "fsdp"),
        P(("fsdp", "ctx"), None),
    )
    out_specs = (
        P(("fsdp", "ctx"), None),
        P(("fsdp", "ctx"), None),
        P("fsdp"),
        P("fsdp", "tensor"),
        P("fsdp", "tensor"),
        P("fsdp", "tensor"),
        P("tensor", "fsdp"),
        P("fsdp"),
        P("fsdp", "tensor"),
        P("fsdp", "tensor"),
        P("tensor", "fsdp"),
    )
    return jax.shard_map(body, mesh=mesh, in_specs=in_specs, out_specs=out_specs, check_vma=False)
```

```python
import math

import jax
import jax.numpy as jnp
from jax import lax
from jax.sharding import PartitionSpec as P

HD = 64
MAXLEN = 512

eps_norm = 1e-05
rope_base = 500000.0

BF = jnp.bfloat16
F32 = jnp.float32


def layout(lengths, token_index):
    seq_ends = jnp.cumsum(lengths, axis=1)
    passed = (token_index[None, :, None] >= seq_ends[:, None, :]).astype(jnp.int32)
    segment = jnp.sum(passed, axis=2)
    seq_start = jnp.sum(passed * lengths[:, None, :], axis=2)
    return segment, token_index[None, :] - seq_start


def rope_tables(position):
    half_width = HD // 2
    frequency = rope_base ** (-jnp.arange(half_width, dtype=F32) / half_width)
    angles = position.astype(F32)[:, None] * frequency[None, :]
    return jnp.cos(angles), jnp.sin(angles)


def rotate(vectors, cosine_table, sine_table, direction):
    half_width = HD // 2
    first_half = vectors[..., :half_width]
    second = vectors[..., half_width:]
    cos_rows = cosine_table[:, None, :]
    sin_rows = direction * sine_table[:, None, :]
    return jnp.concatenate(
        [first_half * cos_rows - second * sin_rows, second * cos_rows + first_half * sin_rows],
        axis=-1,
    )


def norm_forward(rows_wide):
    inv_rms = lax.rsqrt(jnp.mean(rows_wide * rows_wide, axis=-1, keepdims=True) + eps_norm)
    return rows_wide * inv_rms, inv_rms


def norm_backward(delta_rows, unit_rows, inv_rms, gain_wide):
    scaled = gain_wide[None, :] * delta_rows
    gain_term = jnp.sum(delta_rows * unit_rows, axis=0)
    back_term = inv_rms * (
        scaled - unit_rows * jnp.mean(scaled * unit_rows, axis=-1, keepdims=True)
    )
    return gain_term, back_term


def dot(a, b):
    return jnp.dot(a, b, preferred_element_type=F32)


def dot_t(a, b):
    return lax.dot_general(a, b, (((0,), (0,)), ((), ())), preferred_element_type=F32)


def dot_bt(a, b):
    return lax.dot_general(a, b, (((1,), (1,)), ((), ())), preferred_element_type=F32)


def after(value, *deps):
    return lax.optimization_barrier((value,) + deps)[0] if deps else value


def body(
    block_input,
    seq_lengths,
    attn_gain,
    w_query,
    w_key,
    w_value,
    w_output,
    mlp_gain,
    w_gate,
    w_up,
    w_down,
    cotangent,
):
    rows, width = block_input.shape
    n_fsdp, n_ctx, n_ten = (lax.axis_size(a) for a in ("fsdp", "ctx", "tensor"))
    heads_local = w_query.shape[1] // HD
    kv_local = w_key.shape[1] // HD
    tp = math.gcd(n_fsdp, kv_local)
    n_out = n_fsdp // tp
    hq, hk = heads_local // tp, kv_local // tp
    share = hq // hk
    ff_part = w_gate.shape[1] // tp
    d_blk = w_query.shape[0]
    score_scale = 1.0 / math.sqrt(HD)
    i = lax.axis_index("fsdp")
    j = i % tp
    z = lax.axis_index("ctx")
    outer_groups = [[o * tp + jj for o in range(n_out)] for jj in range(tp)]
    bits = []
    b = tp // 2
    while b:
        bits.append(b)
        b //= 2

    lanes = {}

    def send(lane, v, axis, perm):
        out = lax.ppermute(after(v, *lanes.get(lane, ())), axis, perm)
        if lane is not None:
            lanes[lane] = (out,)
        return out

    def swap(v, r):
        return send("x" if r > 1 else None, v, "fsdp", [(s, s ^ r) for s in range(n_fsdp)])

    def free_swap(v, r):
        return lax.ppermute(v, "fsdp", [(s, s ^ r) for s in range(n_fsdp)])

    def shift(v, s, first=0, last=None):
        last = n_ctx if last is None else last
        return lax.ppermute(
            v, "ctx", [(k, k + s) for k in range(first, last) if 0 <= k + s < n_ctx]
        )

    def gather_rows(v):
        for bit in bits:
            v = jnp.concatenate([v, swap(v, bit)], axis=0)
        return v

    def ten_sum(acc):
        low = acc.astype(BF)
        if n_ten == 1:
            return low.astype(F32)
        if n_ten == 2:
            return low.astype(F32) + lax.ppermute(low, "tensor", [(0, 1), (1, 0)]).astype(F32)
        return lax.psum(low, "tensor").astype(F32)

    def reduce_rows(pairs, mult, *deps):
        total = tp * rows
        half = total // 2 if tp > 1 else total
        own = sum(mult(a[:half], w) for a, w in pairs)
        if tp > 1:
            part = after(sum(mult(a[half:], w) for a, w in pairs).astype(BF), *deps)
            own = own + swap(part, bits[-1]).astype(F32)
        for bit in reversed(bits[:-1]):
            half //= 2
            own = own[:half] + swap(own[half:].astype(BF), bit).astype(F32)
        return ten_sum(own)

    def place(buffer, value, start, axis):
        starts = [0] * buffer.ndim
        starts[axis] = start
        return lax.dynamic_update_slice(buffer, value, starts)

    def fetch_near(piece, axis, *deps):
        got = [(piece(j), j)]
        if tp == 4 and n_ctx % 2 == 0:
            odd = z % 2
            perm = [
                (s * n_ctx + k, (s ^ (2 + k % 2)) * n_ctx + k)
                for s in range(n_fsdp)
                for k in range(n_ctx)
            ]
            got.append(
                (send("x", after(piece(j ^ (2 + odd)), *deps), ("fsdp", "ctx"), perm), j ^ (2 + odd))
            )
            got.append((swap(piece(j ^ 1), 1), j ^ 1))
        else:
            got += [(swap(piece(j ^ r), r), j ^ r) for r in range(1, tp)]
        return got, axis

    def fetch_far(state):
        got, axis = state
        if len(got) < tp:
            value, k = got[1]
            got = got + [(send("z", value, "ctx", [(a, a ^ 1) for a in range(n_ctx)]), k ^ 1)]
        size = got[0][0].shape[axis]
        shape = list(got[0][0].shape)
        shape[axis] = tp * size
        full = jnp.zeros(shape, BF)
        for value, k in got:
            full = place(full, value, k * size, axis)
        if n_out > 1:
            full = lax.all_gather(full, "fsdp", axis=axis, tiled=True, axis_index_groups=outer_groups)
        return full

    def cols(w, k, size):
        return lax.dynamic_slice_in_dim(w, k * size, size, axis=1)

    def take_rows(w, k, size):
        return lax.dynamic_slice_in_dim(w, k * size, size, axis=0)

    gains = jnp.stack([attn_gain, mlp_gain])
    gain_all = place(jnp.zeros((2, tp * d_blk), BF), gains, j * d_blk, 1)
    for r in range(1, tp):
        gain_all = place(gain_all, free_swap(gains, r), (j ^ r) * d_blk, 1)
    if n_out > 1:
        gain_all = lax.all_gather(gain_all, "fsdp", axis=1, tiled=True, axis_index_groups=outer_groups)
    gain_one = gain_all[0].astype(F32)
    gain_two = gain_all[1].astype(F32)
    lengths = seq_lengths
    for bit in bits:
        lengths = jnp.concatenate([lengths, free_swap(lengths, bit)], axis=0)

    qkv_state = fetch_near(
        lambda k: jnp.concatenate(
            [cols(w_query, k, hq * HD), cols(w_key, k, hk * HD), cols(w_value, k, hk * HD)], axis=1
        ),
        0,
    )
    input_wide = block_input.astype(F32)
    unit_one, rstd_one = norm_forward(input_wide)
    own_normed = (unit_one * gain_one[None, :]).astype(BF)
    normed_one = gather_rows(own_normed)
    qkv_full = fetch_far(qkv_state)
    out_state = fetch_near(lambda k: take_rows(w_output, k, hq * HD), 1)
    out_full = fetch_far(out_state)
    gate_state = fetch_near(lambda k: cols(w_gate, k, ff_part), 0)

    qkv = dot(normed_one, qkv_full)
    local_index = z * rows + jnp.arange(rows, dtype=jnp.int32)
    q_seg, q_pos = layout(lengths, local_index)
    cosine_table, sine_table = rope_tables(q_pos.reshape(tp * rows))
    q_cols, k_cols = hq * HD, hk * HD
    query_rot = rotate(
        qkv[:, :q_cols].reshape(tp * rows, hq, HD), cosine_table, sine_table, 1.0
    ).astype(BF)
    key_rot = rotate(
        qkv[:, q_cols : q_cols + k_cols].reshape(tp * rows, hk, HD), cosine_table, sine_table, 1.0
    ).astype(BF)
    value_rows = qkv[:, q_cols + k_cols :].astype(BF)

    reach = min(-(-(MAXLEN - 1) // rows), n_ctx - 1)
    kv_own = jnp.concatenate([key_rot.reshape(tp * rows, k_cols), value_rows], axis=1)
    kv_send = after(kv_own, *lanes.get("z", ()))
    kv_blocks = [kv_own] + [shift(kv_send, s) for s in range(1, reach + 1)]
    lanes["z"] = tuple(kv_blocks[1:])
    up_state = fetch_near(lambda k: cols(w_up, k, ff_part), 0, *kv_blocks[1:])
    gate_full = fetch_far(gate_state)
    kv_all = jnp.concatenate(
        [v.reshape(tp, 1, rows, 2, hk, HD) for v in kv_blocks], axis=1
    ).reshape(tp, (reach + 1) * rows, 2, hk, HD)
    key_index = jnp.concatenate(
        [(z - s) * rows + jnp.arange(rows, dtype=jnp.int32) for s in range(reach + 1)]
    )
    k_seg, _ = layout(lengths, key_index)
    allowed = (
        (q_seg[:, :, None] == k_seg[:, None, :])
        & (key_index[None, None, :] <= local_index[None, :, None])
        & (key_index[None, None, :] >= 0)
    )[:, None, None]
    q_h = query_rot.reshape(tp, rows, hk, share, HD).transpose(0, 2, 3, 1, 4)
    k_h = kv_all[:, :, 0].transpose(0, 2, 1, 3)
    v_h = kv_all[:, :, 1].transpose(0, 2, 1, 3)

    q_h = after(q_h, gate_state[0][1][0])
    scores = jnp.einsum("bgrtd,bgsd->bgrts", q_h, k_h, preferred_element_type=F32) * score_scale
    masked = jnp.where(allowed, scores, -1e30)
    row_max = jnp.max(masked, axis=-1, keepdims=True)
    exp_total = jnp.sum(jnp.where(allowed, jnp.exp(masked - row_max), 0.0), axis=-1, keepdims=True)
    log_total = row_max + jnp.log(exp_total)
    prob = jnp.where(allowed, jnp.exp(masked - log_total), 0.0)
    prob_low = prob.astype(BF)
    attended = jnp.einsum("bgrts,bgsd->bgrtd", prob_low, v_h, preferred_element_type=F32).astype(BF)
    attended_rows = attended.transpose(0, 3, 1, 2, 4).reshape(tp * rows, hq * HD)
    half = ff_part // 2
    attended_rows = after(attended_rows, up_state[0][1][0])
    up_full = fetch_far(up_state)
    residual = input_wide + reduce_rows([(attended_rows, out_full)], dot)

    cot_state = [cotangent]
    for bit in bits:
        cot_state.append(swap(jnp.concatenate(cot_state, axis=0), bit))
    cot_all = jnp.concatenate(cot_state, axis=0)
    low_state = fetch_near(lambda k: lax.dynamic_slice_in_dim(w_down, k * ff_part, half, axis=0), 1)
    residual = after(residual, cot_state[1])
    unit_two, rstd_two = norm_forward(residual)
    own_normed_two = (unit_two * gain_two[None, :]).astype(BF)
    normed_two = gather_rows(own_normed_two)
    high_state = fetch_near(
        lambda k: lax.dynamic_slice_in_dim(w_down, k * ff_part + half, half, axis=0), 1
    )
    down_full = jnp.concatenate([fetch_far(low_state), fetch_far(high_state)], axis=0)
    gate_pre = dot(normed_two, gate_full)
    up_pre = dot(normed_two, up_full)
    sigmoid_gate = jax.nn.sigmoid(gate_pre)
    silu_gate = gate_pre * sigmoid_gate
    activation = (silu_gate * up_pre).astype(BF)
    act_delta = dot_bt(cot_all, down_full)
    silu_slope = sigmoid_gate * (1.0 + gate_pre * (1.0 - sigmoid_gate))
    gate_delta = (act_delta * up_pre * silu_slope).astype(BF)
    up_delta = (act_delta * silu_gate).astype(BF)

    mid = n_ctx // 2

    def ctx_total(part):
        acc = part
        for h in range(mid - 1):
            come = send(("in", h), acc, "ctx", [(h, h + 1), (n_ctx - 1 - h, n_ctx - 2 - h)])
            acc = (part.astype(F32) + come.astype(F32)).astype(BF)
        come = send("mid", acc, "ctx", [(mid - 1, mid), (mid, mid - 1)])
        value = (acc.astype(F32) + come.astype(F32)).astype(BF)
        for h in reversed(range(mid - 1)):
            come = send(("out", h), value, "ctx", [(h + 1, h), (n_ctx - 2 - h, n_ctx - 1 - h)])
            value = jnp.where((z == h) | (z == n_ctx - 1 - h), come, value)
        return value

    def exchange(piece, lane):
        held, out = lanes.get(lane, ()), [(j, piece(j))]
        for r in range(1, tp):
            out.append((j ^ r, free_swap(after(piece(j ^ r), *(held if r > 1 else ())), r)))
        if lane is not None and tp > 2:
            lanes[lane] = tuple(value for _, value in out[2:])
        return out

    def finish_rows(view, widths):
        _, b, c = view.shape
        if n_out > 1:
            view = lax.psum_scatter(
                view.reshape(n_out, tp, b, c), "fsdp", scatter_dimension=0, axis_index_groups=outer_groups
            )
        got = exchange(lambda k: lax.dynamic_slice_in_dim(view, k, 1, axis=0)[0], "x")
        mine = jnp.zeros((b, tp * c), BF)
        base = low = 0
        for w in widths:
            for k, value in got:
                mine = lax.dynamic_update_slice(mine, value[:, low : low + w], (0, base + k * w))
            base, low = base + tp * w, low + w
        return mine

    def finish_cols(part):
        b = part.shape[0]
        if n_out > 1:
            part = lax.psum_scatter(
                part.reshape(b, n_out, tp * d_blk), "fsdp", scatter_dimension=1, axis_index_groups=outer_groups
            )
        got = exchange(lambda k: cols(part, k, d_blk), "x")
        mine = jnp.zeros((tp, b, d_blk), BF)
        for k, value in got:
            mine = lax.dynamic_update_slice(mine, value[None], (k, 0, 0))
        return mine

    def grad_cols(left, right, n, chunks):
        b = left.shape[1] // chunks
        return finish_cols(dot_t(left[:, n * b : (n + 1) * b], right).astype(BF))

    def grad_rows(part, widths, n, chunks):
        b = d_blk // chunks
        return finish_rows(part.reshape(n_fsdp, chunks, b, part.shape[1])[:, n], widths)

    def join_cols(done):
        full = jnp.stack([v.astype(F32) for v in done], axis=1)
        return full.reshape(-1, d_blk)

    def join_rows(done):
        return jnp.concatenate([v.astype(F32) for v in done], axis=0)

    up_part = dot_t(normed_two, up_delta).astype(BF)
    gate_part = dot_t(normed_two, gate_delta).astype(BF)
    down_low_grad = ctx_total(grad_cols(activation, cot_all, 0, 2))
    normed_two_delta = reduce_rows([(gate_delta, gate_full), (up_delta, up_full)], dot_bt)
    down_high_grad = ctx_total(grad_cols(activation, cot_all, 1, 2))
    gain_two_term, residual_back = norm_backward(normed_two_delta, unit_two, rstd_two, gain_two)
    residual_delta = cotangent.astype(F32) + residual_back
    up_low_grad = ctx_total(grad_rows(up_part, (ff_part,), 0, 2))
    residual_low = gather_rows(residual_delta.astype(BF))
    up_high_grad = ctx_total(grad_rows(up_part, (ff_part,), 1, 2))
    gate_low_grad = ctx_total(grad_rows(gate_part, (ff_part,), 0, 2))
    output_grad = ctx_total(grad_cols(attended_rows, residual_low, 0, 1))
    gate_high_grad = ctx_total(grad_rows(gate_part, (ff_part,), 1, 2))

    attended_delta = dot_bt(residual_low, out_full).astype(BF)
    delta_h = attended_delta.reshape(tp, rows, hk, share, HD).transpose(0, 2, 3, 1, 4)
    inner_rows = jnp.sum(attended.astype(F32) * delta_h.astype(F32), axis=-1, keepdims=True)
    prob_delta = jnp.einsum("bgrtd,bgsd->bgrts", delta_h, v_h, preferred_element_type=F32)
    score_delta = (prob * (prob_delta - inner_rows) * score_scale).astype(BF)
    query_back = jnp.einsum("bgrts,bgsd->bgrtd", score_delta, k_h, preferred_element_type=F32)
    key_back = jnp.einsum("bgrts,bgrtd->bgsd", score_delta, q_h, preferred_element_type=F32)
    value_back = jnp.einsum("bgrts,bgrtd->bgsd", prob_low, delta_h, preferred_element_type=F32)

    def to_blocks(v):
        v = v.transpose(0, 2, 1, 3).reshape(tp, reach + 1, rows, k_cols)
        return [v[:, s].reshape(tp * rows, k_cols) for s in range(reach + 1)]

    kv_back = [
        jnp.concatenate([kb, vb], axis=1) for kb, vb in zip(to_blocks(key_back), to_blocks(value_back))
    ]
    kv_sum = kv_back[0]
    for s in range(1, reach + 1):
        kv_sum = kv_sum + shift(kv_back[s].astype(BF), -s).astype(F32)
    query_delta = rotate(
        query_back.transpose(0, 3, 1, 2, 4).reshape(tp * rows, hq, HD), cosine_table, sine_table, -1.0
    ).reshape(tp * rows, q_cols)
    key_delta = rotate(
        kv_sum[:, :k_cols].reshape(tp * rows, hk, HD), cosine_table, sine_table, -1.0
    ).reshape(tp * rows, k_cols)
    qkv_delta = jnp.concatenate([query_delta, key_delta, kv_sum[:, k_cols:]], axis=1).astype(BF)
    qkv_part = dot_t(normed_one, qkv_delta).astype(BF)
    qkv_out = join_rows(
        [ctx_total(grad_rows(qkv_part, (q_cols, k_cols, k_cols), n, 2)) for n in range(2)]
    )
    normed_one_delta = reduce_rows([(qkv_delta, qkv_full)], dot_bt)
    block_output = (residual + reduce_rows([(activation, down_full)], dot)).astype(BF)
    gain_one_term, input_back = norm_backward(normed_one_delta, unit_one, rstd_one, gain_one)
    input_grad = residual_delta + input_back

    terms = jnp.stack([gain_one_term, gain_two_term])
    if n_out > 1:
        terms = lax.psum_scatter(
            terms.reshape(2, n_out, tp * d_blk), "fsdp", scatter_dimension=1, axis_index_groups=outer_groups
        )
    got = exchange(lambda k: cols(terms, k, d_blk), None)
    gain_sum = sum(value for _, value in got)
    step = 1
    while step < n_ctx:
        gain_sum = gain_sum + lax.ppermute(gain_sum, "ctx", [(k, k ^ step) for k in range(n_ctx)])
        step *= 2
    gain_grads = gain_sum

    q_all, k_all = tp * q_cols, tp * k_cols
    return (
        block_output,
        input_grad,
        gain_grads[0],
        qkv_out[:, :q_all],
        qkv_out[:, q_all : q_all + k_all],
        qkv_out[:, q_all + k_all :],
        join_cols([output_grad]),
        gain_grads[1],
        join_rows([gate_low_grad, gate_high_grad]),
        join_rows([up_low_grad, up_high_grad]),
        join_cols([down_low_grad, down_high_grad]),
    )


def solution(mesh):
    in_specs = (
        P(("fsdp", "ctx"), None),
        P("fsdp", None),
        P("fsdp"),
        P("fsdp", "tensor"),
        P("fsdp", "tensor"),
        P("fsdp", "tensor"),
        P("tensor", "fsdp"),
        P("fsdp"),
        P("fsdp", "tensor"),
        P("fsdp", "tensor"),
        P("tensor", "fsdp"),
        P(("fsdp", "ctx"), None),
    )
    out_specs = (
        P(("fsdp", "ctx"), None),
        P(("fsdp", "ctx"), None),
        P("fsdp"),
        P("fsdp", "tensor"),
        P("fsdp", "tensor"),
        P("fsdp", "tensor"),
        P("tensor", "fsdp"),
        P("fsdp"),
        P("fsdp", "tensor"),
        P("fsdp", "tensor"),
        P("tensor", "fsdp"),
    )
    return jax.shard_map(body, mesh=mesh, in_specs=in_specs, out_specs=out_specs, check_vma=False)
```

```python
import math

import jax
import jax.numpy as jnp
from jax import lax
from jax.sharding import PartitionSpec as P


HD = 64
MAXLEN = 512

eps_norm = 1e-05
rope_base = 500000.0

BF = jnp.bfloat16
F32 = jnp.float32


def layout(lengths, token_index):
    seq_ends = jnp.cumsum(lengths, axis=1)
    passed = (token_index[None, :, None] >= seq_ends[:, None, :]).astype(jnp.int32)
    segment = jnp.sum(passed, axis=2)
    seq_start = jnp.sum(passed * lengths[:, None, :], axis=2)
    return segment, token_index[None, :] - seq_start


def rope_tables(position):
    half_width = HD // 2
    frequency = rope_base ** (-jnp.arange(half_width, dtype=F32) / half_width)
    angles = position.astype(F32)[:, None] * frequency[None, :]
    return jnp.cos(angles), jnp.sin(angles)


def rotate(vectors, cosine_table, sine_table, direction):
    half_width = HD // 2
    first_half = vectors[..., :half_width]
    second = vectors[..., half_width:]
    cos_rows = cosine_table[:, None, :]
    sin_rows = direction * sine_table[:, None, :]
    return jnp.concatenate(
        [first_half * cos_rows - second * sin_rows, second * cos_rows + first_half * sin_rows],
        axis=-1,
    )


def norm_forward(rows_wide):
    inv_rms = lax.rsqrt(jnp.mean(rows_wide * rows_wide, axis=-1, keepdims=True) + eps_norm)
    return rows_wide * inv_rms, inv_rms


def norm_backward(delta_rows, unit_rows, inv_rms, gain_wide):
    scaled = gain_wide[None, :] * delta_rows
    gain_term = jnp.sum(delta_rows * unit_rows, axis=0)
    back_term = inv_rms * (
        scaled - unit_rows * jnp.mean(scaled * unit_rows, axis=-1, keepdims=True)
    )
    return gain_term, back_term


def dot(a, b):
    return jnp.dot(a, b, preferred_element_type=F32)


def dot_t(a, b):
    return lax.dot_general(a, b, (((0,), (0,)), ((), ())), preferred_element_type=F32)


def dot_bt(a, b):
    return lax.dot_general(a, b, (((1,), (1,)), ((), ())), preferred_element_type=F32)


def after(value, *deps):
    return lax.optimization_barrier((value,) + deps)[0] if deps else value


def body(
    block_input,
    seq_lengths,
    attn_gain,
    w_query,
    w_key,
    w_value,
    w_output,
    mlp_gain,
    w_gate,
    w_up,
    w_down,
    cotangent,
):
    rows, _ = block_input.shape
    n_fsdp, n_ctx, n_ten = (lax.axis_size(a) for a in ("fsdp", "ctx", "tensor"))
    heads_local = w_query.shape[1] // HD
    kv_local = w_key.shape[1] // HD
    tp = math.gcd(n_fsdp, kv_local)
    n_out = n_fsdp // tp
    hq, hk = heads_local // tp, kv_local // tp
    share = hq // hk
    ff_part = w_gate.shape[1] // tp
    d_blk = w_query.shape[0]
    score_scale = 1.0 / math.sqrt(HD)
    i = lax.axis_index("fsdp")
    j = i % tp
    z = lax.axis_index("ctx")
    outer_groups = [[o * tp + jj for o in range(n_out)] for jj in range(tp)]
    bits = []
    b = tp // 2
    while b:
        bits.append(b)
        b //= 2

    lanes = {}

    def send(lane, v, axis, perm, depth=1):
        line = lanes.setdefault(lane, []) if lane is not None else []
        held = line[-depth] if len(line) >= depth else ()
        out = lax.ppermute(after(v, *held), axis, perm)
        line.append((out,))
        return out

    def swap(v, r, lane=None):
        return send(lane if r > 1 else None, v, "fsdp", [(s, s ^ r) for s in range(n_fsdp)])

    def shift(v, s):
        pairs = [(k, k + s) for k in range(n_ctx) if 0 <= k + s < n_ctx]
        return send(None, v, "ctx", pairs)

    def gather_rows(v, lane=None):
        for bit in bits:
            v = jnp.concatenate([v, swap(v, bit, lane)], axis=0)
        return v

    def ten_sum(acc):
        low = acc.astype(BF)
        if n_ten == 1:
            return low.astype(F32)
        if n_ten == 2:
            other = send(None, low, "tensor", [(0, 1), (1, 0)])
            return low.astype(F32) + other.astype(F32)
        return lax.psum(low, "tensor").astype(F32)

    def reduce_rows(pairs, mult, lane=None):
        total = tp * rows
        half = total // 2 if tp > 1 else total
        own = sum(mult(a[:half], w) for a, w in pairs)
        if tp > 1:
            part = sum(mult(a[half:], w) for a, w in pairs).astype(BF)
            own = own + swap(part, bits[-1]).astype(F32)
        for bit in reversed(bits[:-1]):
            half //= 2
            own = own[:half] + swap(own[half:].astype(BF), bit, lane).astype(F32)
        return ten_sum(own)

    def place(buffer, value, start, axis):
        starts = [0] * buffer.ndim
        starts[axis] = start
        return lax.dynamic_update_slice(buffer, value, starts)

    def fetch_near(piece, axis, name):
        got = [(piece(j), j)]
        if tp == 4 and n_ctx % 2 == 0:
            odd = z % 2
            perm = [
                (s * n_ctx + k, (s ^ (2 + k % 2)) * n_ctx + k)
                for s in range(n_fsdp)
                for k in range(n_ctx)
            ]
            far = send(None, piece(j ^ (2 + odd)), ("fsdp", "ctx"), perm)
            got.append((far, j ^ (2 + odd)))
            got.append((swap(piece(j ^ 1), 1), j ^ 1))
        else:
            got += [(swap(piece(j ^ r), r), j ^ r) for r in range(1, tp)]
        return got, axis, name

    def fetch_far(state):
        got, axis, _ = state
        if len(got) < tp:
            value, k = got[1]
            value = send(None, value, "ctx", [(a, a ^ 1) for a in range(n_ctx)])
            got = got + [(value, k ^ 1)]
        size = got[0][0].shape[axis]
        shape = list(got[0][0].shape)
        shape[axis] = tp * size
        full = jnp.zeros(shape, BF)
        for value, k in got:
            full = place(full, value, k * size, axis)
        if n_out > 1:
            full = lax.all_gather(full, "fsdp", axis=axis, tiled=True, axis_index_groups=outer_groups)
        return full

    def cols(w, k, size):
        return lax.dynamic_slice_in_dim(w, k * size, size, axis=1)

    def take_rows(w, k, size):
        return lax.dynamic_slice_in_dim(w, k * size, size, axis=0)

    gains = jnp.stack([attn_gain, mlp_gain])
    gain_all = place(jnp.zeros((2, tp * d_blk), BF), gains, j * d_blk, 1)
    for r in range(1, tp):
        gain_all = place(gain_all, swap(gains, r), (j ^ r) * d_blk, 1)
    if n_out > 1:
        gain_all = lax.all_gather(gain_all, "fsdp", axis=1, tiled=True, axis_index_groups=outer_groups)
    gain_one = gain_all[0].astype(F32)
    gain_two = gain_all[1].astype(F32)
    lengths = seq_lengths
    for bit in bits:
        lengths = jnp.concatenate([lengths, swap(lengths, bit)], axis=0)

    qkv_state = fetch_near(
        lambda k: jnp.concatenate(
            [cols(w_query, k, hq * HD), cols(w_key, k, hk * HD), cols(w_value, k, hk * HD)], axis=1
        ),
        0,
        "wqkv",
    )
    input_wide = block_input.astype(F32)
    unit_one, rstd_one = norm_forward(input_wide)
    own_normed = (unit_one * gain_one[None, :]).astype(BF)
    normed_one = gather_rows(own_normed)
    qkv_full = fetch_far(qkv_state)
    half = ff_part // 2
    out_full = fetch_far(fetch_near(lambda k: take_rows(w_output, k, hq * HD), 1, "wo"))
    gate_full = fetch_far(fetch_near(lambda k: cols(w_gate, k, ff_part), 0, "wg"))
    up_full = fetch_far(fetch_near(lambda k: cols(w_up, k, ff_part), 0, "wu"))
    down_full = jnp.concatenate(
        [
            fetch_far(
                fetch_near(
                    lambda k: lax.dynamic_slice_in_dim(w_down, k * ff_part + at, half, axis=0), 1, name
                )
            )
            for at, name in ((0, "wl"), (half, "wh"))
        ],
        axis=0,
    )

    qkv = dot(normed_one, qkv_full)
    local_index = z * rows + jnp.arange(rows, dtype=jnp.int32)
    q_seg, q_pos = layout(lengths, local_index)
    cosine_table, sine_table = rope_tables(q_pos.reshape(tp * rows))
    q_cols, k_cols = hq * HD, hk * HD
    query_rot = rotate(
        qkv[:, :q_cols].reshape(tp * rows, hq, HD), cosine_table, sine_table, 1.0
    ).astype(BF)
    key_rot = rotate(
        qkv[:, q_cols : q_cols + k_cols].reshape(tp * rows, hk, HD), cosine_table, sine_table, 1.0
    ).astype(BF)
    value_rows = qkv[:, q_cols + k_cols :].astype(BF)

    reach = min(-(-(MAXLEN - 1) // rows), n_ctx - 1)
    kv_own = jnp.concatenate([key_rot.reshape(tp * rows, k_cols), value_rows], axis=1)
    kv_blocks = [kv_own] + [shift(kv_own, s) for s in range(1, reach + 1)]
    kv_all = jnp.concatenate(
        [v.reshape(tp, 1, rows, 2, hk, HD) for v in kv_blocks], axis=1
    ).reshape(tp, (reach + 1) * rows, 2, hk, HD)
    key_index = jnp.concatenate(
        [(z - s) * rows + jnp.arange(rows, dtype=jnp.int32) for s in range(reach + 1)]
    )
    k_seg, _ = layout(lengths, key_index)
    allowed = (
        (q_seg[:, :, None] == k_seg[:, None, :])
        & (key_index[None, None, :] <= local_index[None, :, None])
        & (key_index[None, None, :] >= 0)
    )[:, None, None]
    q_h = query_rot.reshape(tp, rows, hk, share, HD).transpose(0, 2, 3, 1, 4)
    k_h = kv_all[:, :, 0].transpose(0, 2, 1, 3)
    v_h = kv_all[:, :, 1].transpose(0, 2, 1, 3)

    scores = jnp.einsum("bgrtd,bgsd->bgrts", q_h, k_h, preferred_element_type=F32) * score_scale
    masked = jnp.where(allowed, scores, -1e30)
    row_max = jnp.max(masked, axis=-1, keepdims=True)
    exp_total = jnp.sum(jnp.where(allowed, jnp.exp(masked - row_max), 0.0), axis=-1, keepdims=True)
    log_total = row_max + jnp.log(exp_total)
    prob = jnp.where(allowed, jnp.exp(masked - log_total), 0.0)
    prob_low = prob.astype(BF)
    attended = jnp.einsum("bgrts,bgsd->bgrtd", prob_low, v_h, preferred_element_type=F32).astype(BF)
    attended_rows = attended.transpose(0, 3, 1, 2, 4).reshape(tp * rows, hq * HD)
    residual = input_wide + reduce_rows([(attended_rows, out_full)], dot)

    cot_all = gather_rows(cotangent)
    unit_two, rstd_two = norm_forward(residual)
    normed_two = gather_rows((unit_two * gain_two[None, :]).astype(BF))
    gate_pre = dot(normed_two, gate_full)
    up_pre = dot(normed_two, up_full)
    sigmoid_gate = jax.nn.sigmoid(gate_pre)
    silu_gate = gate_pre * sigmoid_gate
    activation = (silu_gate * up_pre).astype(BF)
    act_delta = dot_bt(cot_all, down_full)
    silu_slope = sigmoid_gate * (1.0 + gate_pre * (1.0 - sigmoid_gate))
    gate_delta = (act_delta * up_pre * silu_slope).astype(BF)
    up_delta = (act_delta * silu_gate).astype(BF)

    mid = n_ctx // 2

    def ctx_total(part):
        acc = part
        for h in range(mid - 1):
            pairs = [(h, h + 1), (n_ctx - 1 - h, n_ctx - 2 - h)]
            come = send(("in", h), acc, "ctx", pairs, 2)
            acc = (part.astype(F32) + come.astype(F32)).astype(BF)
        come = send("mid", acc, "ctx", [(mid - 1, mid), (mid, mid - 1)], 2)
        value = (acc.astype(F32) + come.astype(F32)).astype(BF)
        for h in reversed(range(mid - 1)):
            pairs = [(h + 1, h), (n_ctx - 2 - h, n_ctx - 1 - h)]
            come = send(("out", h), value, "ctx", pairs, 2)
            value = jnp.where((z == h) | (z == n_ctx - 1 - h), come, value)
        return value

    def exchange(piece, lane):
        line = lanes.setdefault(lane, []) if lane is not None else []
        held, out = (line[-1] if line else ()), [(j, piece(j))]
        for r in range(1, tp):
            out.append((j ^ r, swap(after(piece(j ^ r), *(held if r > 1 else ())), r)))
        line.append(tuple(value for _, value in out[2:]))
        return out

    def finish_rows(view, widths):
        _, b, c = view.shape
        if n_out > 1:
            view = lax.psum_scatter(
                view.reshape(n_out, tp, b, c), "fsdp", scatter_dimension=0, axis_index_groups=outer_groups
            )
        got = exchange(lambda k: lax.dynamic_slice_in_dim(view, k, 1, axis=0)[0], "x")
        mine = jnp.zeros((b, tp * c), BF)
        base = low = 0
        for w in widths:
            for k, value in got:
                mine = lax.dynamic_update_slice(mine, value[:, low : low + w], (0, base + k * w))
            base, low = base + tp * w, low + w
        return mine

    def finish_cols(part):
        b = part.shape[0]
        if n_out > 1:
            part = lax.psum_scatter(
                part.reshape(b, n_out, tp * d_blk), "fsdp", scatter_dimension=1, axis_index_groups=outer_groups
            )
        got = exchange(lambda k: cols(part, k, d_blk), "x")
        mine = jnp.zeros((tp, b, d_blk), BF)
        for k, value in got:
            mine = lax.dynamic_update_slice(mine, value[None], (k, 0, 0))
        return mine

    def grad_cols(left, right, n, chunks):
        b = left.shape[1] // chunks
        return finish_cols(dot_t(left[:, n * b : (n + 1) * b], right).astype(BF))

    def grad_rows(part, widths, n, chunks):
        b = d_blk // chunks
        return finish_rows(part.reshape(n_fsdp, chunks, b, part.shape[1])[:, n], widths)

    def join_cols(done):
        full = jnp.stack([v.astype(F32) for v in done], axis=1)
        return full.reshape(-1, d_blk)

    def join_rows(done):
        return jnp.concatenate([v.astype(F32) for v in done], axis=0)

    up_part = dot_t(normed_two, up_delta).astype(BF)
    gate_part = dot_t(normed_two, gate_delta).astype(BF)
    down_low_grad = ctx_total(grad_cols(activation, cot_all, 0, 2))
    down_high_grad = ctx_total(grad_cols(activation, cot_all, 1, 2))
    normed_two_delta = reduce_rows([(gate_delta, gate_full), (up_delta, up_full)], dot_bt, "x")
    gain_two_term, residual_back = norm_backward(normed_two_delta, unit_two, rstd_two, gain_two)
    residual_delta = cotangent.astype(F32) + residual_back
    up_low_grad = ctx_total(grad_rows(up_part, (ff_part,), 0, 2))
    residual_low = gather_rows(residual_delta.astype(BF), "x")
    up_high_grad = ctx_total(grad_rows(up_part, (ff_part,), 1, 2))
    gate_low_grad = ctx_total(grad_rows(gate_part, (ff_part,), 0, 2))
    output_grad = ctx_total(grad_cols(attended_rows, residual_low, 0, 1))
    gate_high_grad = ctx_total(grad_rows(gate_part, (ff_part,), 1, 2))

    attended_delta = dot_bt(residual_low, out_full).astype(BF)
    delta_h = attended_delta.reshape(tp, rows, hk, share, HD).transpose(0, 2, 3, 1, 4)
    inner_rows = jnp.sum(attended.astype(F32) * delta_h.astype(F32), axis=-1, keepdims=True)
    prob_delta = jnp.einsum("bgrtd,bgsd->bgrts", delta_h, v_h, preferred_element_type=F32)
    score_delta = (prob * (prob_delta - inner_rows) * score_scale).astype(BF)
    query_back = jnp.einsum("bgrts,bgsd->bgrtd", score_delta, k_h, preferred_element_type=F32)
    key_back = jnp.einsum("bgrts,bgrtd->bgsd", score_delta, q_h, preferred_element_type=F32)
    value_back = jnp.einsum("bgrts,bgrtd->bgsd", prob_low, delta_h, preferred_element_type=F32)

    def to_blocks(v):
        v = v.transpose(0, 2, 1, 3).reshape(tp, reach + 1, rows, k_cols)
        return [v[:, s].reshape(tp * rows, k_cols) for s in range(reach + 1)]

    kv_back = [
        jnp.concatenate([kb, vb], axis=1) for kb, vb in zip(to_blocks(key_back), to_blocks(value_back))
    ]
    kv_sum = kv_back[0]
    for s in range(1, reach + 1):
        kv_sum = kv_sum + shift(kv_back[s].astype(BF), -s).astype(F32)
    query_delta = rotate(
        query_back.transpose(0, 3, 1, 2, 4).reshape(tp * rows, hq, HD), cosine_table, sine_table, -1.0
    ).reshape(tp * rows, q_cols)
    key_delta = rotate(
        kv_sum[:, :k_cols].reshape(tp * rows, hk, HD), cosine_table, sine_table, -1.0
    ).reshape(tp * rows, k_cols)
    qkv_delta = jnp.concatenate([query_delta, key_delta, kv_sum[:, k_cols:]], axis=1).astype(BF)
    qkv_part = dot_t(normed_one, qkv_delta).astype(BF)
    qkv_out = join_rows(
        [ctx_total(grad_rows(qkv_part, (q_cols, k_cols, k_cols), n, 2)) for n in range(2)]
    )
    normed_one_delta = reduce_rows([(qkv_delta, qkv_full)], dot_bt, "x")
    block_output = (residual + reduce_rows([(activation, down_full)], dot, "x")).astype(BF)
    gain_one_term, input_back = norm_backward(normed_one_delta, unit_one, rstd_one, gain_one)
    input_grad = residual_delta + input_back

    terms = jnp.stack([gain_one_term, gain_two_term])
    if n_out > 1:
        terms = lax.psum_scatter(
            terms.reshape(2, n_out, tp * d_blk), "fsdp", scatter_dimension=1, axis_index_groups=outer_groups
        )
    got = exchange(lambda k: cols(terms, k, d_blk), None)
    gain_sum = sum(value for _, value in got)
    step = 1
    while step < n_ctx:
        gain_sum = gain_sum + lax.ppermute(gain_sum, "ctx", [(k, k ^ step) for k in range(n_ctx)])
        step *= 2
    gain_grads = gain_sum

    q_all, k_all = tp * q_cols, tp * k_cols
    return (
        block_output,
        input_grad,
        gain_grads[0],
        qkv_out[:, :q_all],
        qkv_out[:, q_all : q_all + k_all],
        qkv_out[:, q_all + k_all :],
        join_cols([output_grad]),
        gain_grads[1],
        join_rows([gate_low_grad, gate_high_grad]),
        join_rows([up_low_grad, up_high_grad]),
        join_cols([down_low_grad, down_high_grad]),
    )


def solution(mesh):
    in_specs = (
        P(("fsdp", "ctx"), None),
        P("fsdp", None),
        P("fsdp"),
        P("fsdp", "tensor"),
        P("fsdp", "tensor"),
        P("fsdp", "tensor"),
        P("tensor", "fsdp"),
        P("fsdp"),
        P("fsdp", "tensor"),
        P("fsdp", "tensor"),
        P("tensor", "fsdp"),
        P(("fsdp", "ctx"), None),
    )
    out_specs = (
        P(("fsdp", "ctx"), None),
        P(("fsdp", "ctx"), None),
        P("fsdp"),
        P("fsdp", "tensor"),
        P("fsdp", "tensor"),
        P("fsdp", "tensor"),
        P("tensor", "fsdp"),
        P("fsdp"),
        P("fsdp", "tensor"),
        P("fsdp", "tensor"),
        P("tensor", "fsdp"),
    )

    return jax.shard_map(body, mesh=mesh, in_specs=in_specs, out_specs=out_specs, check_vma=False)
```

```python
import math

import jax
import jax.numpy as jnp
from jax import lax
from jax.experimental import pallas as pl
from jax.sharding import PartitionSpec as P


HD = 64
MAXLEN = 512

eps_norm = 1e-05
rope_base = 500000.0

BF = jnp.bfloat16
F32 = jnp.float32


def layout(lengths, token_index):
    seq_ends = jnp.cumsum(lengths, axis=1)
    passed = (token_index[None, :, None] >= seq_ends[:, None, :]).astype(jnp.int32)
    segment = jnp.sum(passed, axis=2)
    seq_start = jnp.sum(passed * lengths[:, None, :], axis=2)
    return segment, token_index[None, :] - seq_start


def rope_tables(position):
    half_width = HD // 2
    frequency = rope_base ** (-jnp.arange(half_width, dtype=F32) / half_width)
    angles = position.astype(F32)[:, None] * frequency[None, :]
    return jnp.cos(angles), jnp.sin(angles)


def rotate(vectors, cosine_table, sine_table, direction):
    half_width = HD // 2
    first_half = vectors[..., :half_width]
    second = vectors[..., half_width:]
    cos_rows = cosine_table[:, None, :]
    sin_rows = direction * sine_table[:, None, :]
    return jnp.concatenate(
        [first_half * cos_rows - second * sin_rows, second * cos_rows + first_half * sin_rows],
        axis=-1,
    )


def norm_forward(rows_wide):
    inv_rms = lax.rsqrt(jnp.mean(rows_wide * rows_wide, axis=-1, keepdims=True) + eps_norm)
    return rows_wide * inv_rms, inv_rms


def norm_backward(delta_rows, unit_rows, inv_rms, gain_wide):
    scaled = gain_wide[None, :] * delta_rows
    gain_term = jnp.sum(delta_rows * unit_rows, axis=0)
    back_term = inv_rms * (
        scaled - unit_rows * jnp.mean(scaled * unit_rows, axis=-1, keepdims=True)
    )
    return gain_term, back_term


def dot(a, b):
    return jnp.dot(a, b, preferred_element_type=F32)


def dot_t(a, b):
    return lax.dot_general(a, b, (((0,), (0,)), ((), ())), preferred_element_type=F32)


def dot_bt(a, b):
    return lax.dot_general(a, b, (((1,), (1,)), ((), ())), preferred_element_type=F32)


def visible(qseg_ref, kseg_ref, rows, n):
    qseg = qseg_ref[0]
    out = [qseg == kseg_ref[0, s : s + 1, :] for s in range(n)]
    at = lax.broadcasted_iota(jnp.int32, (rows, rows), 0)
    to = lax.broadcasted_iota(jnp.int32, (rows, rows), 1)
    out[0] = out[0] & (to <= at)
    return out


def attention_forward(q, kvs, qseg, kseg, hq, hk, score_scale):
    groups, rows, _ = qseg.shape
    n, share, kw = len(kvs), hq // hk, hk * HD

    def kernel(q_ref, *refs):
        kv_refs, (qseg_ref, kseg_ref, o_ref, lse_ref) = refs[:n], refs[n:]
        seen = visible(qseg_ref, kseg_ref, rows, n)
        outs, lses = [], []
        for h in range(hq):
            g = h // share
            qh = q_ref[:, h * HD : (h + 1) * HD]
            scores = [
                jnp.where(
                    seen[s], dot_bt(qh, kv_refs[s][:, g * HD : (g + 1) * HD]) * score_scale, -1e30
                )
                for s in range(n)
            ]
            top = scores[0].max(-1, keepdims=True)
            for s in range(1, n):
                top = jnp.maximum(top, scores[s].max(-1, keepdims=True))
            weights = [jnp.exp(sc - top) for sc in scores]
            total = sum(w.sum(-1, keepdims=True) for w in weights)
            scale = 1.0 / total
            outs.append(
                sum(
                    dot((weights[s] * scale).astype(BF), kv_refs[s][:, kw + g * HD : kw + (g + 1) * HD])
                    for s in range(n)
                )
            )
            lses.append(top + jnp.log(total))
        o_ref[...] = jnp.concatenate(outs, axis=1).astype(BF)
        lse_ref[0] = jnp.concatenate(lses, axis=1)

    return pl.pallas_call(
        kernel,
        grid=(groups,),
        in_specs=[pl.BlockSpec((rows, hq * HD), lambda b: (b, 0))]
        + [pl.BlockSpec((rows, 2 * kw), lambda b: (b, 0))] * n
        + [
            pl.BlockSpec((1, rows, 1), lambda b: (b, 0, 0)),
            pl.BlockSpec((1, n, rows), lambda b: (b, 0, 0)),
        ],
        out_specs=[
            pl.BlockSpec((rows, hq * HD), lambda b: (b, 0)),
            pl.BlockSpec((1, rows, hq), lambda b: (b, 0, 0)),
        ],
        out_shape=[
            jax.ShapeDtypeStruct((groups * rows, hq * HD), BF),
            jax.ShapeDtypeStruct((groups, rows, hq), F32),
        ],
        name="attention_forward",
    )(q, *kvs, qseg, kseg)


def attention_backward(q, kvs, qseg, kseg, lse, attended, delta, hq, hk, score_scale):
    groups, rows, _ = qseg.shape
    n, share, kw = len(kvs), hq // hk, hk * HD

    def kernel(q_ref, *refs):
        kv_refs = refs[:n]
        qseg_ref, kseg_ref, lse_ref, o_ref, d_ref, dq_ref = refs[n : n + 6]
        dkv_refs = refs[n + 6 :]
        seen = visible(qseg_ref, kseg_ref, rows, n)
        dqs = []
        back = [[[0.0] * hk, [0.0] * hk] for _ in range(n)]
        for h in range(hq):
            g, own = h // share, slice(h * HD, (h + 1) * HD)
            qh, dh = q_ref[:, own], d_ref[:, own]
            inner = jnp.sum(o_ref[:, own].astype(F32) * dh.astype(F32), axis=-1, keepdims=True)
            log_total = lse_ref[0, :, h : h + 1]
            dq = 0.0
            for s in range(n):
                key = kv_refs[s][:, g * HD : (g + 1) * HD]
                value = kv_refs[s][:, kw + g * HD : kw + (g + 1) * HD]
                scores = jnp.where(seen[s], dot_bt(qh, key) * score_scale, -1e30)
                prob = jnp.exp(scores - log_total)
                grad = (prob * (dot_bt(dh, value) - inner) * score_scale).astype(BF)
                dq = dq + dot(grad, key)
                back[s][0][g] = back[s][0][g] + dot_t(grad, qh)
                back[s][1][g] = back[s][1][g] + dot_t(prob.astype(BF), dh)
            dqs.append(dq)
        dq_ref[...] = jnp.concatenate(dqs, axis=1)
        for s in range(n):
            dkv_refs[s][...] = jnp.concatenate(back[s][0] + back[s][1], axis=1).astype(
                dkv_refs[s].dtype
            )

    wide = pl.BlockSpec((rows, hq * HD), lambda b: (b, 0))
    pair = pl.BlockSpec((rows, 2 * kw), lambda b: (b, 0))
    return pl.pallas_call(
        kernel,
        grid=(groups,),
        in_specs=[wide]
        + [pair] * n
        + [
            pl.BlockSpec((1, rows, 1), lambda b: (b, 0, 0)),
            pl.BlockSpec((1, n, rows), lambda b: (b, 0, 0)),
            pl.BlockSpec((1, rows, hq), lambda b: (b, 0, 0)),
            wide,
            wide,
        ],
        out_specs=[wide] + [pair] * n,
        out_shape=[jax.ShapeDtypeStruct((groups * rows, hq * HD), F32)]
        + [
            jax.ShapeDtypeStruct((groups * rows, 2 * kw), F32 if s == 0 else BF) for s in range(n)
        ],
        name="attention_backward",
    )(q, *kvs, qseg, kseg, lse, attended, delta)


def after(value, *deps):
    return lax.optimization_barrier((value,) + deps)[0] if deps else value


def body(
    block_input,
    seq_lengths,
    attn_gain,
    w_query,
    w_key,
    w_value,
    w_output,
    mlp_gain,
    w_gate,
    w_up,
    w_down,
    cotangent,
):
    rows, _ = block_input.shape
    n_fsdp, n_ctx, n_ten = (lax.axis_size(a) for a in ("fsdp", "ctx", "tensor"))
    heads_local = w_query.shape[1] // HD
    kv_local = w_key.shape[1] // HD
    tp = math.gcd(n_fsdp, kv_local)
    n_out = n_fsdp // tp
    hq, hk = heads_local // tp, kv_local // tp
    ff_part = w_gate.shape[1] // tp
    d_blk = w_query.shape[0]
    score_scale = 1.0 / math.sqrt(HD)
    i = lax.axis_index("fsdp")
    j = i % tp
    z = lax.axis_index("ctx")
    outer_groups = [[o * tp + jj for o in range(n_out)] for jj in range(tp)]
    bits = []
    b = tp // 2
    while b:
        bits.append(b)
        b //= 2

    lanes = {}

    def send(lane, v, axis, perm, depth=1):
        line = lanes.setdefault(lane, []) if lane is not None else []
        held = line[-depth] if len(line) >= depth else ()
        out = lax.ppermute(after(v, *held), axis, perm)
        line.append((out,))
        return out

    def swap(v, r, lane=None):
        return send(lane if r > 1 else None, v, "fsdp", [(s, s ^ r) for s in range(n_fsdp)])

    def shift(v, s):
        pairs = [(k, k + s) for k in range(n_ctx) if 0 <= k + s < n_ctx]
        return send(None, v, "ctx", pairs)

    def gather_rows(v, lane=None):
        for bit in bits:
            v = jnp.concatenate([v, swap(v, bit, lane)], axis=0)
        return v

    def ten_sum(acc):
        low = acc.astype(BF)
        if n_ten == 1:
            return low.astype(F32)
        if n_ten == 2:
            other = send(None, low, "tensor", [(0, 1), (1, 0)])
            return low.astype(F32) + other.astype(F32)
        return lax.psum(low, "tensor").astype(F32)

    def reduce_rows(pairs, mult, lane=None):
        total = tp * rows
        half = total // 2 if tp > 1 else total
        own = sum(mult(a[:half], w) for a, w in pairs)
        if tp > 1:
            part = sum(mult(a[half:], w) for a, w in pairs).astype(BF)
            own = own + swap(part, bits[-1]).astype(F32)
        for bit in reversed(bits[:-1]):
            half //= 2
            own = own[:half] + swap(own[half:].astype(BF), bit, lane).astype(F32)
        return ten_sum(own)

    def place(buffer, value, start, axis):
        starts = [0] * buffer.ndim
        starts[axis] = start
        return lax.dynamic_update_slice(buffer, value, starts)

    def fetch_near(piece, axis, name):
        got = [(piece(j), j)]
        if tp == 4 and n_ctx % 2 == 0:
            odd = z % 2
            perm = [
                (s * n_ctx + k, (s ^ (2 + k % 2)) * n_ctx + k)
                for s in range(n_fsdp)
                for k in range(n_ctx)
            ]
            far = send(None, piece(j ^ (2 + odd)), ("fsdp", "ctx"), perm)
            got.append((far, j ^ (2 + odd)))
            got.append((swap(piece(j ^ 1), 1), j ^ 1))
        else:
            got += [(swap(piece(j ^ r), r), j ^ r) for r in range(1, tp)]
        return got, axis, name

    def fetch_far(state):
        got, axis, _ = state
        if len(got) < tp:
            value, k = got[1]
            value = send(None, value, "ctx", [(a, a ^ 1) for a in range(n_ctx)])
            got = got + [(value, k ^ 1)]
        size = got[0][0].shape[axis]
        shape = list(got[0][0].shape)
        shape[axis] = tp * size
        full = jnp.zeros(shape, BF)
        for value, k in got:
            full = place(full, value, k * size, axis)
        if n_out > 1:
            full = lax.all_gather(full, "fsdp", axis=axis, tiled=True, axis_index_groups=outer_groups)
        return full

    def cols(w, k, size):
        return lax.dynamic_slice_in_dim(w, k * size, size, axis=1)

    def take_rows(w, k, size):
        return lax.dynamic_slice_in_dim(w, k * size, size, axis=0)

    gains = jnp.stack([attn_gain, mlp_gain])
    gain_all = place(jnp.zeros((2, tp * d_blk), BF), gains, j * d_blk, 1)
    for r in range(1, tp):
        gain_all = place(gain_all, swap(gains, r), (j ^ r) * d_blk, 1)
    if n_out > 1:
        gain_all = lax.all_gather(gain_all, "fsdp", axis=1, tiled=True, axis_index_groups=outer_groups)
    gain_one = gain_all[0].astype(F32)
    gain_two = gain_all[1].astype(F32)
    lengths = seq_lengths
    for bit in bits:
        lengths = jnp.concatenate([lengths, swap(lengths, bit)], axis=0)

    qkv_state = fetch_near(
        lambda k: jnp.concatenate(
            [cols(w_query, k, hq * HD), cols(w_key, k, hk * HD), cols(w_value, k, hk * HD)], axis=1
        ),
        0,
        "wqkv",
    )
    input_wide = block_input.astype(F32)
    unit_one, rstd_one = norm_forward(input_wide)
    own_normed = (unit_one * gain_one[None, :]).astype(BF)
    normed_one = gather_rows(own_normed)
    qkv_full = fetch_far(qkv_state)
    half = ff_part // 2
    out_full = fetch_far(fetch_near(lambda k: take_rows(w_output, k, hq * HD), 1, "wo"))
    gate_full = fetch_far(fetch_near(lambda k: cols(w_gate, k, ff_part), 0, "wg"))
    up_full = fetch_far(fetch_near(lambda k: cols(w_up, k, ff_part), 0, "wu"))
    down_full = jnp.concatenate(
        [
            fetch_far(
                fetch_near(
                    lambda k: lax.dynamic_slice_in_dim(w_down, k * ff_part + at, half, axis=0), 1, name
                )
            )
            for at, name in ((0, "wl"), (half, "wh"))
        ],
        axis=0,
    )

    qkv = dot(normed_one, qkv_full)
    local_index = z * rows + jnp.arange(rows, dtype=jnp.int32)
    q_seg, q_pos = layout(lengths, local_index)
    cosine_table, sine_table = rope_tables(q_pos.reshape(tp * rows))
    q_cols, k_cols = hq * HD, hk * HD
    query_rot = rotate(
        qkv[:, :q_cols].reshape(tp * rows, hq, HD), cosine_table, sine_table, 1.0
    ).astype(BF)
    key_rot = rotate(
        qkv[:, q_cols : q_cols + k_cols].reshape(tp * rows, hk, HD), cosine_table, sine_table, 1.0
    ).astype(BF)
    value_rows = qkv[:, q_cols + k_cols :].astype(BF)

    reach = min(-(-(MAXLEN - 1) // rows), n_ctx - 1)
    kv_own = jnp.concatenate([key_rot.reshape(tp * rows, k_cols), value_rows], axis=1)
    kv_blocks = [kv_own] + [shift(kv_own, s) for s in range(1, reach + 1)]
    key_index = jnp.concatenate(
        [(z - s) * rows + jnp.arange(rows, dtype=jnp.int32) for s in range(reach + 1)]
    )
    k_seg, _ = layout(lengths, key_index)
    k_seg = jnp.where(key_index[None, :] >= 0, k_seg, -1).reshape(tp, reach + 1, rows)
    q_seg = q_seg[:, :, None]
    query_rows = query_rot.reshape(tp * rows, q_cols)
    attended_rows, log_total = attention_forward(
        query_rows, kv_blocks, q_seg, k_seg, hq, hk, score_scale
    )
    residual = input_wide + reduce_rows([(attended_rows, out_full)], dot)

    cot_all = gather_rows(cotangent)
    unit_two, rstd_two = norm_forward(residual)
    normed_two = gather_rows((unit_two * gain_two[None, :]).astype(BF))
    gate_pre = dot(normed_two, gate_full)
    up_pre = dot(normed_two, up_full)
    sigmoid_gate = jax.nn.sigmoid(gate_pre)
    silu_gate = gate_pre * sigmoid_gate
    activation = (silu_gate * up_pre).astype(BF)
    down_parts = [
        dot_t(activation[:, at : at + half], cot_all).astype(BF) for at in range(0, ff_part, half)
    ]
    act_delta = dot_bt(cot_all, after(down_full, *down_parts))
    silu_slope = sigmoid_gate * (1.0 + gate_pre * (1.0 - sigmoid_gate))
    gate_delta = (act_delta * up_pre * silu_slope).astype(BF)
    up_delta = (act_delta * silu_gate).astype(BF)

    mid = n_ctx // 2

    def ctx_total(part):
        acc = part
        for h in range(mid - 1):
            pairs = [(h, h + 1), (n_ctx - 1 - h, n_ctx - 2 - h)]
            come = send(("in", h), acc, "ctx", pairs, 2)
            acc = (part.astype(F32) + come.astype(F32)).astype(BF)
        come = send("mid", acc, "ctx", [(mid - 1, mid), (mid, mid - 1)], 2)
        value = (acc.astype(F32) + come.astype(F32)).astype(BF)
        for h in reversed(range(mid - 1)):
            pairs = [(h + 1, h), (n_ctx - 2 - h, n_ctx - 1 - h)]
            come = send(("out", h), value, "ctx", pairs, 2)
            value = jnp.where((z == h) | (z == n_ctx - 1 - h), come, value)
        return value

    def exchange(piece, lane):
        line = lanes.setdefault(lane, []) if lane is not None else []
        held, out = (line[-1] if line else ()), [(j, piece(j))]
        for r in range(1, tp):
            out.append((j ^ r, swap(after(piece(j ^ r), *(held if r > 1 else ())), r)))
        line.append(tuple(value for _, value in out[2:]))
        return out

    def finish_rows(view, widths):
        _, b, c = view.shape
        if n_out > 1:
            view = lax.psum_scatter(
                view.reshape(n_out, tp, b, c), "fsdp", scatter_dimension=0, axis_index_groups=outer_groups
            )
        got = exchange(lambda k: lax.dynamic_slice_in_dim(view, k, 1, axis=0)[0], "x")
        mine = jnp.zeros((b, tp * c), BF)
        base = low = 0
        for w in widths:
            for k, value in got:
                mine = lax.dynamic_update_slice(mine, value[:, low : low + w], (0, base + k * w))
            base, low = base + tp * w, low + w
        return mine

    def finish_cols(part):
        b = part.shape[0]
        if n_out > 1:
            part = lax.psum_scatter(
                part.reshape(b, n_out, tp * d_blk), "fsdp", scatter_dimension=1, axis_index_groups=outer_groups
            )
        got = exchange(lambda k: cols(part, k, d_blk), "x")
        mine = jnp.zeros((tp, b, d_blk), BF)
        for k, value in got:
            mine = lax.dynamic_update_slice(mine, value[None], (k, 0, 0))
        return mine

    def grad_rows(part, widths, n, chunks):
        b = d_blk // chunks
        return finish_rows(part.reshape(n_fsdp, chunks, b, part.shape[1])[:, n], widths)

    def join_cols(done):
        full = jnp.stack([v.astype(F32) for v in done], axis=1)
        return full.reshape(-1, d_blk)

    def join_rows(done):
        return jnp.concatenate([v.astype(F32) for v in done], axis=0)

    up_part = dot_t(normed_two, up_delta).astype(BF)
    gate_part = dot_t(normed_two, gate_delta).astype(BF)
    down_grads = [ctx_total(finish_cols(part)) for part in down_parts]
    normed_two_delta = reduce_rows([(gate_delta, gate_full), (up_delta, up_full)], dot_bt, "x")
    gain_two_term, residual_back = norm_backward(normed_two_delta, unit_two, rstd_two, gain_two)
    residual_delta = cotangent.astype(F32) + residual_back
    up_grads = [ctx_total(grad_rows(up_part, (ff_part,), n, 2)) for n in range(2)]
    residual_low = gather_rows(residual_delta.astype(BF), "x")
    gate_grads = [ctx_total(grad_rows(gate_part, (ff_part,), n, 2)) for n in range(2)]
    output_grad = ctx_total(finish_cols(dot_t(attended_rows, residual_low).astype(BF)))

    attended_delta = dot_bt(residual_low, out_full).astype(BF)
    query_back, *kv_back = attention_backward(
        query_rows, kv_blocks, q_seg, k_seg, log_total, attended_rows, attended_delta,
        hq, hk, score_scale,
    )
    kv_sum = kv_back[0]
    for s in range(1, reach + 1):
        kv_sum = kv_sum + shift(kv_back[s], -s).astype(F32)
    query_delta = rotate(
        query_back.reshape(tp * rows, hq, HD), cosine_table, sine_table, -1.0
    ).reshape(tp * rows, q_cols)
    key_delta = rotate(
        kv_sum[:, :k_cols].reshape(tp * rows, hk, HD), cosine_table, sine_table, -1.0
    ).reshape(tp * rows, k_cols)
    qkv_delta = jnp.concatenate([query_delta, key_delta, kv_sum[:, k_cols:]], axis=1).astype(BF)
    qkv_part = dot_t(normed_one, qkv_delta).astype(BF)
    qkv_out = join_rows(
        [ctx_total(grad_rows(qkv_part, (q_cols, k_cols, k_cols), n, 2)) for n in range(2)]
    )
    normed_one_delta = reduce_rows([(qkv_delta, qkv_full)], dot_bt, "x")
    block_output = (residual + reduce_rows([(activation, down_full)], dot, "x")).astype(BF)
    gain_one_term, input_back = norm_backward(normed_one_delta, unit_one, rstd_one, gain_one)
    input_grad = residual_delta + input_back

    terms = jnp.stack([gain_one_term, gain_two_term])
    if n_out > 1:
        terms = lax.psum_scatter(
            terms.reshape(2, n_out, tp * d_blk), "fsdp", scatter_dimension=1, axis_index_groups=outer_groups
        )
    got = exchange(lambda k: cols(terms, k, d_blk), None)
    gain_sum = after(sum(value for _, value in got), *lanes["mid"][-1])
    step = 1
    while step < n_ctx:
        gain_sum = gain_sum + lax.ppermute(gain_sum, "ctx", [(k, k ^ step) for k in range(n_ctx)])
        step *= 2
    gain_grads = gain_sum

    q_all, k_all = tp * q_cols, tp * k_cols
    return (
        block_output,
        input_grad,
        gain_grads[0],
        qkv_out[:, :q_all],
        qkv_out[:, q_all : q_all + k_all],
        qkv_out[:, q_all + k_all :],
        join_cols([output_grad]),
        gain_grads[1],
        join_rows(gate_grads),
        join_rows(up_grads),
        join_cols(down_grads),
    )


def solution(mesh):
    in_specs = (
        P(("fsdp", "ctx"), None),
        P("fsdp", None),
        P("fsdp"),
        P("fsdp", "tensor"),
        P("fsdp", "tensor"),
        P("fsdp", "tensor"),
        P("tensor", "fsdp"),
        P("fsdp"),
        P("fsdp", "tensor"),
        P("fsdp", "tensor"),
        P("tensor", "fsdp"),
        P(("fsdp", "ctx"), None),
    )
    out_specs = (
        P(("fsdp", "ctx"), None),
        P(("fsdp", "ctx"), None),
        P("fsdp"),
        P("fsdp", "tensor"),
        P("fsdp", "tensor"),
        P("fsdp", "tensor"),
        P("tensor", "fsdp"),
        P("fsdp"),
        P("fsdp", "tensor"),
        P("fsdp", "tensor"),
        P("tensor", "fsdp"),
    )

    return jax.shard_map(body, mesh=mesh, in_specs=in_specs, out_specs=out_specs, check_vma=False)
```
